32 devices in a mesh: dp: 8 (over z, x), seq: 4 (over y, core).
Axes of the slice: x: 2, y: 2, z: 4, core: 2. Of those that a mesh axis runs over, the one named last changes fastest.
Arguments:
- tokens: bfloat16 [96, 512, 768], P('dp', 'seq'), may hold values from -6 to 6
- lengths: int32 [96], P('dp'), may hold values from 20 to 512, as said below
- cotangent: bfloat16 [96, 512, 768], P('dp', 'seq'), may hold values from -6 to 6
- w_query: bfloat16 [768, 768], replicated, may hold values from -0.21875 to 0.21875
- w_key: bfloat16 [768, 768], replicated, may hold values from -0.21875 to 0.21875
- w_value: bfloat16 [768, 768], replicated, may hold values from -0.21875 to 0.21875
- w_out: bfloat16 [768, 768], replicated, may hold values from -0.875 to 0.875
- w_inner: bfloat16 [768, 3072], replicated, may hold values from -0.21875 to 0.21875
- w_outer: bfloat16 [3072, 768], replicated, may hold values from -0.109375 to 0.109375
- down_one: bfloat16 [768, 64], replicated, may hold values from -0.21875 to 0.21875
- up_one: bfloat16 [64, 768], replicated, may hold values from -0.75 to 0.75
- down_two: bfloat16 [768, 64], replicated, may hold values from -0.21875 to 0.21875
- up_two: bfloat16 [64, 768], replicated, may hold values from -0.75 to 0.75
- gain_one: float32 [768], replicated, may hold values from 0.5 to 1.5
- bias_one: float32 [768], replicated, may hold values from -3 to 3
- gain_two: float32 [768], replicated, may hold values from 0.5 to 1.5
- bias_two: float32 [768], replicated, may hold values from -3 to 3
Outputs:
- output: bfloat16 [96, 512, 768], P('dp', 'seq')
- input_grad: float32 [96, 512, 768], P('dp', 'seq')
- grad_down_one: float32 [768, 64], replicated
- grad_up_one: float32 [64, 768], replicated
- grad_down_two: float32 [768, 64], replicated
- grad_up_two: float32 [64, 768], replicated
- grad_gain_one: float32 [768], replicated
- grad_bias_one: float32 [768], replicated
- grad_gain_two: float32 [768], replicated
- grad_bias_two: float32 [768], replicated
The draws below stay inside these ranges and needn't reach their ends.
Inputs may be any that keep to these rules, and one draw needn't show every extreme that they name: `lengths`: among the 12 sequences of each index of dp, one has exactly 512 tokens and another exactly 20.
All inputs are finite; a program needn't handle non-finite values.
Results may differ from the reference program's by a relative error of at most 0.015.
Values may be sent and summed in bfloat16 or wider, within the bound.
A program may use at most 320 MiB of HBM per device.

```python
import jax
import jax.numpy as jnp
from jax import lax

D = 768
HEADS = 12
HEAD = 64
FF = 3072
ADAPT = 64
LEN = 512
SEQ_DEV = 12
SL = 128
SEQS = 96
N_SEQ = 4


def draw_lengths(key, part):
    groups = SEQS // SEQ_DEV
    key_upper, key_raw, key_long, key_short = jax.random.split(key, 4)
    upper = jax.random.randint(key_upper, (groups, 1), min(LEN, max(LEN // 4, 24)), LEN + 1)
    raw = jax.random.randint(key_raw, (groups, SEQ_DEV), 0, 1 << 20)
    values = 20 + raw % (upper - 19)
    index = jnp.arange(SEQ_DEV).reshape(1, SEQ_DEV)
    longest = jax.random.randint(key_long, (groups, 1), 0, SEQ_DEV)
    offset = jax.random.randint(key_short, (groups, 1), 0, SEQ_DEV - 1)
    shortest = (longest + 1 + offset) % SEQ_DEV
    values = jnp.where(index == longest, LEN, values)
    values = jnp.where(index == shortest, 20, values)
    return values.reshape(SEQS).astype(jnp.int32)


def levels(key, shape, shards, low, largest):
    level, own = 1.0, jax.random.fold_in(key, 6)
    for axis_at, blocks in shards:
        steps = jnp.exp(jax.random.uniform(jax.random.fold_in(own, axis_at), (blocks,), jnp.float32, low / len(shards), largest / len(shards)))
        level = level * jnp.repeat(steps, shape[axis_at] // blocks).reshape([-1 if axis == axis_at else 1 for axis in range(len(shape))])
    return level


def scatter_about(rng, shape, width, reach, cuts=(), dtype=jnp.bfloat16):
    loudness = levels(rng, shape, cuts, -0.22, 0.18) if cuts else 1.0
    values = jax.random.normal(rng, shape, jnp.float32) * width * loudness
    return jnp.minimum(jnp.maximum(values, -reach), reach).astype(dtype)


def setup_inputs(seed: int = 0) -> dict:
    key_of = jax.random.split(jax.random.key(seed), 18)
    tokens = scatter_about(key_of[0], (SEQS, LEN, D), 1.0, 6.0, ((0, 8), (1, 4)))
    lengths = draw_lengths(jax.random.fold_in(key_of[17], 71), 0)
    cotangent = scatter_about(key_of[2], (SEQS, LEN, D), 1.0, 6.0, ((0, 8), (1, 4)))
    w_query = scatter_about(key_of[3], (D, D), D ** -0.5, 0.21875)
    w_key = scatter_about(key_of[4], (D, D), D ** -0.5, 0.21875)
    w_value = scatter_about(key_of[5], (D, D), D ** -0.5, 0.21875)
    w_out = scatter_about(key_of[6], (D, D), (D // 16) ** -0.5, 0.875)
    w_inner = scatter_about(key_of[7], (D, FF), D ** -0.5, 0.21875)
    w_outer = scatter_about(key_of[8], (FF, D), FF ** -0.5, 0.109375)
    down_one = scatter_about(key_of[9], (D, ADAPT), D ** -0.5, 0.21875)
    up_one = scatter_about(key_of[10], (ADAPT, D), ADAPT ** -0.5, 0.75)
    down_two = scatter_about(key_of[11], (D, ADAPT), D ** -0.5, 0.21875)
    up_two = scatter_about(key_of[12], (ADAPT, D), ADAPT ** -0.5, 0.75)
    gain_one = jnp.clip(1.0 + 0.1 * jax.random.normal(key_of[13], (D,), jnp.float32), 0.5, 1.5)
    bias_one = scatter_about(key_of[14], (D,), 0.5, 3.0, (), jnp.float32)
    gain_two = jnp.clip(1.0 + 0.1 * jax.random.normal(key_of[15], (D,), jnp.float32), 0.5, 1.5)
    bias_two = scatter_about(key_of[16], (D,), 0.5, 3.0, (), jnp.float32)
    return {"tokens": tokens, "lengths": lengths, "cotangent": cotangent, "w_query": w_query, "w_key": w_key, "w_value": w_value, "w_out": w_out, "w_inner": w_inner, "w_outer": w_outer, "down_one": down_one, "up_one": up_one, "down_two": down_two, "up_two": up_two, "gain_one": gain_one, "bias_one": bias_one, "gain_two": gain_two, "bias_two": bias_two}


@jax.custom_vjp
def low(v):
    return lax.optimization_barrier(v.astype(jnp.bfloat16)).astype(jnp.float32)

@jax.custom_vjp
def low_back(v):
    return v

def low_keep(v):
    return (low(v), None)

def low_pass(kept, grad):
    return (grad,)

def back_keep(v):
    return (v, None)

def back_low(kept, grad):
    return (low(grad),)
low.defvjp(low_keep, low_pass)
low_back.defvjp(back_keep, back_low)
EPS = 1e-06
HIGH = lax.Precision.HIGHEST

def matmul(left, right):
    return jnp.dot(left, right, precision=HIGH)

def layer_norm(hidden, gain, bias):
    mean = lax.optimization_barrier(jnp.mean(hidden, axis=-1, keepdims=True))
    centred = hidden - mean
    inverse = lax.rsqrt(lax.optimization_barrier(jnp.mean(centred * centred, axis=-1, keepdims=True)) + EPS)
    return centred * inverse * gain + bias

def gelu_exact(value):
    return jax.nn.gelu(value, approximate=False)

def attention(query, key, value, valid):
    queries = query.reshape(LEN, HEADS, HEAD)
    keys = key.reshape(N_SEQ, SL, HEADS, HEAD)
    values = value.reshape(N_SEQ, SL, HEADS, HEAD)
    scores = low_back(jnp.einsum('qhd,nkhd->hqnk', queries, keys, precision=HIGH) * HEAD ** (-0.5))
    mask = valid[None, None]
    masked = jnp.where(mask, scores, -1e+30)
    top = lax.optimization_barrier(jnp.max(masked, axis=3, keepdims=True))
    expo = jnp.where(mask, jnp.exp(masked - top), 0.0)
    total = lax.optimization_barrier(jnp.sum(expo, axis=3, keepdims=True))
    peak = lax.optimization_barrier(jnp.max(top, axis=2, keepdims=True))
    weight = jnp.exp(top - peak)
    denom = lax.optimization_barrier(jnp.sum(total * weight, axis=2))
    part = jnp.einsum('hqnk,nkhd->hqnd', low(expo), values, precision=HIGH)
    attn = lax.optimization_barrier(jnp.sum(part * weight, axis=2)) / denom
    return attn.transpose(1, 0, 2).reshape(LEN, D)

def forward(inputs, valid, frozen, train):
    w_query, w_key, w_value, w_out, w_inner, w_outer = frozen
    down_one, up_one, down_two, up_two, gain_one, bias_one, gain_two, bias_two = train
    query = low_back(low(matmul(inputs, w_query)))
    key = low_back(low(matmul(inputs, w_key)))
    value = low_back(low(matmul(inputs, w_value)))
    ctx = low(low_back(attention(query, key, value, valid)))
    out_proj = low_back(matmul(ctx, w_out))
    out_low = low(out_proj)
    zed_one = low_back(matmul(out_low, down_one))
    branch_one = low_back(matmul(low(gelu_exact(zed_one)), up_one))
    hidden_one = inputs + out_proj + branch_one
    normed_one = layer_norm(hidden_one, gain_one, bias_one)
    inner = low_back(matmul(low(normed_one), w_inner))
    ffn_out = low_back(matmul(low(gelu_exact(inner)), w_outer))
    zed_two = low_back(matmul(low(ffn_out), down_two))
    branch_two = low_back(matmul(low(gelu_exact(zed_two)), up_two))
    hidden_two = normed_one + ffn_out + branch_two
    return layer_norm(hidden_two, gain_two, bias_two)

def reference(tokens, lengths, cotangent, w_query, w_key, w_value, w_out, w_inner, w_outer, down_one, up_one, down_two, up_two, gain_one, bias_one, gain_two, bias_two):
    frozen = tuple((w.astype(jnp.float32) for w in (w_query, w_key, w_value, w_out, w_inner, w_outer)))
    train = tuple((w.astype(jnp.float32) for w in (down_one, up_one, down_two, up_two, gain_one, bias_one, gain_two, bias_two)))
    positions = jnp.arange(LEN).reshape(N_SEQ, SL)

    def step(carry, item):
        inputs, length, grad_out = item
        valid = positions < length

        def local(inputs32, params):
            return forward(inputs32, valid, frozen, params)
        result, pull = jax.vjp(local, inputs.astype(jnp.float32), train)
        grad_in, grad_train = pull(grad_out.astype(jnp.float32))
        carry = tuple((c + g for c, g in zip(carry, grad_train)))
        return (carry, (result.astype(jnp.bfloat16), grad_in))
    start = tuple((jnp.zeros_like(w) for w in train))
    sums, (outputs, grads) = lax.scan(step, start, (tokens, lengths, cotangent))
    return (outputs, grads, sums[0], sums[1], sums[2], sums[3], sums[4], sums[5], sums[6], sums[7])
```

```python
import functools

import jax
import jax.numpy as jnp
from jax import lax
from jax.experimental import pallas as pl
from jax.experimental.pallas import tpu as pltpu
from jax.sharding import PartitionSpec as P

HEADS = 12
EPS = 1e-06
F32 = jnp.float32
BF16 = jnp.bfloat16
NN = (((1,), (0,)), ((), ()))
NT = (((1,), (1,)), ((), ()))
TN = (((0,), (0,)), ((), ()))
MESH = pl.DeviceIdType.MESH
LANES = 128
GROUP = 8


def dot(left, right, dims=NN):
    return lax.dot_general(left, right, dims, preferred_element_type=F32)


def gelu_parts(value):
    phi = 0.5 + 0.5 * lax.erf(value * 0.7071067811865476)
    scaled = value * jnp.exp(value * value * -0.5) * 0.3989422804014327
    return value * phi, phi + scaled


def row_mean(value):
    return jnp.sum(value, axis=-1, keepdims=True) * (1.0 / value.shape[-1])


def norm_forward(hidden):
    centred = hidden - row_mean(hidden)
    inverse = lax.rsqrt(row_mean(centred * centred) + EPS)
    return centred * inverse, inverse


def norm_backward(grad, unit, inverse, gain):
    scaled = grad * gain
    inner = scaled - row_mean(scaled) - unit * row_mean(scaled * unit)
    return inner * inverse


class Refs:
    pass


def attend_forward(s, bias):
    span = s.query.shape[1]
    half = span // 2
    low = lax.broadcasted_iota(jnp.int32, (1, LANES), 1) < LANES // 2

    @pl.loop(0, s.query.shape[0])
    def _(pair):
        key, value = s.key[pair], s.value[pair]
        zero = jnp.zeros_like(key)
        keys = (jnp.where(low, key, zero), jnp.where(low, zero, key))
        for block in range(2):
            rows = pl.ds(block * half, half)
            query = s.query[pair, rows, :]
            outs, invs = [], []
            for head in range(2):
                scores = dot(query, keys[head], NT) + bias
                top = jnp.max(scores, axis=-1, keepdims=True)
                expo = jnp.exp(scores - top)
                total = jnp.sum(expo, axis=-1, keepdims=True)
                expo_low = expo.astype(BF16)
                s.expo[2 * pair + head, rows, :] = expo_low
                outs.append(dot(expo_low, value))
                invs.append(1.0 / total)
            inv = jnp.where(low, invs[0], invs[1])
            attn = jnp.where(low, outs[0], outs[1]) * inv
            s.inv[pair, rows, :] = inv
            s.attn[pair, rows, :] = attn
            s.ctx[rows, pl.ds(pl.multiple_of(pair * LANES, LANES), LANES)] = attn.astype(BF16)


def attend_backward(s):
    span = s.query.shape[1]
    half = span // 2
    low = lax.broadcasted_iota(jnp.int32, (1, LANES), 1) < LANES // 2

    @pl.loop(0, s.query.shape[0])
    def _(pair):
        lanes = pl.ds(pl.multiple_of(pair * LANES, LANES), LANES)
        key, value, query = s.key[pair], s.value[pair], s.query[pair]
        zero = jnp.zeros_like(key)
        keys = (jnp.where(low, key, zero), jnp.where(low, zero, key))
        wide = s.ctx[:, lanes].astype(F32) * s.inv[pair]
        terms = wide * s.attn[pair]
        deltas = (
            jnp.sum(jnp.where(low, terms, 0.0), axis=-1, keepdims=True),
            jnp.sum(jnp.where(low, 0.0, terms), axis=-1, keepdims=True),
        )
        grad = wide.astype(BF16)
        grads = (jnp.where(low, grad, zero), jnp.where(low, zero, grad))
        grad_t, query_t = grad.T, query.T
        dquery = [None, None]
        for head in range(2):
            sub = slice(head * LANES // 2, (head + 1) * LANES // 2)
            for block in range(2):
                rows = slice(block * half, (block + 1) * half)
                expo = s.expo[2 * pair + head, pl.ds(block * half, half), :]
                dprob = dot(grads[head][rows], value, NT)
                dscores = (expo.astype(F32) * (dprob - deltas[head][rows])).astype(BF16)
                s.dscores[head, pl.ds(block * half, half), :] = dscores
                part = dot(dscores, keys[head])
                dquery[block] = part if head == 0 else dquery[block] + part
            s.dvalue_t[sub, :] = dot(grad_t[sub], s.expo[2 * pair + head]).astype(BF16)
            s.dkey_t[sub, :] = dot(query_t[sub], s.dscores[head]).astype(BF16)
        scale = (LANES // 2) ** -0.5
        for block in range(2):
            s.dquery[pl.ds(block * half, half), lanes] = (dquery[block] * scale).astype(BF16)
        s.dkey[:, lanes] = s.dkey_t[...].T
        s.dvalue[:, lanes] = s.dvalue_t[...].T


def layer(s, tokens, cotangent, length, before_dy):
    span, width = tokens.shape
    pairs = width // LANES
    tiles = s.w_inner.shape[0]
    block = 256
    blocks = span // block
    scale = (LANES // 2) ** -0.5

    for b in range(blocks):
        rows = pl.ds(b * block, block)
        x = tokens[rows, :]
        for weight, target, factor in (
            (s.w_query, s.query, scale),
            (s.w_key, s.key, None),
            (s.w_value, s.value, None),
        ):
            y = dot(x, weight[...]).astype(BF16)
            if factor is not None:
                y = y * jnp.asarray(factor, BF16)
            for pair in range(pairs):
                target[pair, rows, :] = y[:, pair * LANES : (pair + 1) * LANES]

    position = lax.broadcasted_iota(jnp.int32, (1, span), 1)
    bias = jnp.where(position < length, 0.0, -1e30)
    attend_forward(s, bias)

    for b in range(blocks):
        rows = pl.ds(b * block, block)
        out = dot(s.ctx[rows, :], s.w_out[...])
        out_low = out.astype(BF16)
        s.out_low[rows, :] = out_low
        act, slope = gelu_parts(dot(out_low, s.down_one[...]))
        act = act.astype(BF16)
        s.act_one[rows, :] = act
        s.slope_one[rows, :] = slope
        hidden = tokens[rows, :].astype(F32) + out + dot(act, s.up_one[...])
        unit, inverse = norm_forward(hidden)
        s.unit_one[rows, :] = unit
        s.inverse_one[rows, :] = inverse
        normed = unit * s.gain_one[...] + s.bias_one[...]
        s.normed_low[rows, :] = normed.astype(BF16)
        s.total[rows, :] = jnp.zeros((block, width), F32)

    @pl.loop(0, tiles)
    def _(tile):
        for b in range(blocks):
            rows = pl.ds(b * block, block)
            act, slope = gelu_parts(dot(s.normed_low[rows, :], s.w_inner[tile]))
            s.slope[tile, rows, :] = slope.astype(BF16)
            s.total[rows, :] += dot(act.astype(BF16), s.w_outer[tile])

    before_dy()
    for b in range(blocks):
        rows = pl.ds(b * block, block)
        ffn = s.total[rows, :]
        ffn_low = ffn.astype(BF16)
        act, slope = gelu_parts(dot(ffn_low, s.down_two[...]))
        act = act.astype(BF16)
        normed = s.unit_one[rows, :] * s.gain_one[...] + s.bias_one[...]
        hidden = normed + ffn + dot(act, s.up_two[...])
        unit, inverse = norm_forward(hidden)
        s.output[rows, :] = (unit * s.gain_two[...] + s.bias_two[...]).astype(BF16)
        dy = cotangent[rows, :].astype(F32)
        s.vectors[2:3, :] += jnp.sum(dy * unit, axis=0, keepdims=True)
        s.vectors[3:4, :] += jnp.sum(dy, axis=0, keepdims=True)
        dh = norm_backward(dy, unit, inverse, s.gain_two[...])
        da = dh.astype(BF16)
        s.grads[3] += dot(act, da, TN)
        dz = (dot(da, s.up_two[...], NT) * slope).astype(BF16)
        s.grads[2] += dot(dz, ffn_low, TN)
        s.total[rows, :] = dh
        s.dffn[rows, :] = (dh + dot(dz, s.down_two[...], NT)).astype(BF16)

    @pl.loop(0, tiles)
    def _(tile):
        for b in range(blocks):
            rows = pl.ds(b * block, block)
            du = dot(s.dffn[rows, :], s.w_outer[tile], NT) * s.slope[tile, rows, :].astype(F32)
            s.total[rows, :] += dot(du.astype(BF16), s.w_inner[tile], NT)

    for b in range(blocks):
        rows = pl.ds(b * block, block)
        dy = s.total[rows, :]
        unit = s.unit_one[rows, :]
        s.vectors[0:1, :] += jnp.sum(dy * unit, axis=0, keepdims=True)
        s.vectors[1:2, :] += jnp.sum(dy, axis=0, keepdims=True)
        dh = norm_backward(dy, unit, s.inverse_one[rows, :], s.gain_one[...])
        s.total[rows, :] = dh
        da = dh.astype(BF16)
        s.grads[1] += dot(s.act_one[rows, :], da, TN)
        dz = (dot(da, s.up_one[...], NT) * s.slope_one[rows, :]).astype(BF16)
        s.grads[0] += dot(dz, s.out_low[rows, :], TN)
        dout = (dh + dot(dz, s.down_one[...], NT)).astype(BF16)
        s.ctx[rows, :] = dot(dout, s.w_out[...], NT).astype(BF16)

    attend_backward(s)

    for b in range(blocks):
        rows = pl.ds(b * block, block)
        grad = s.total[rows, :] + dot(s.dquery[rows, :], s.w_query[...], NT)
        grad = grad + dot(s.dkey[rows, :], s.w_key[...], NT)
        grad = grad + dot(s.dvalue[rows, :], s.w_value[...], NT)
        s.grad_in[rows, :] = grad.astype(BF16)


INPUTS = (
    "w_query", "w_key", "w_value", "w_out", "w_inner", "w_outer",
    "down_one", "up_one", "down_two", "up_two",
    "gain_one", "bias_one", "gain_two", "bias_two",
)
BIG = INPUTS[:6]


def layer_scratch(span, width, hidden, adapt):
    pairs, tiles = width // LANES, hidden // width
    v = pltpu.VMEM
    return {
        "w_query": v((width, width), BF16),
        "w_key": v((width, width), BF16),
        "w_value": v((width, width), BF16),
        "w_out": v((width, width), BF16),
        "w_inner": v((tiles, width, width), BF16),
        "w_outer": v((tiles, width, width), BF16),
        "query": v((pairs, span, LANES), BF16),
        "key": v((pairs, span, LANES), BF16),
        "value": v((pairs, span, LANES), BF16),
        "expo": v((2 * pairs, span, span), BF16),
        "inv": v((pairs, span, LANES), F32),
        "attn": v((pairs, span, LANES), F32),
        "ctx": v((span, width), BF16),
        "out_low": v((span, width), BF16),
        "act_one": v((span, adapt), BF16),
        "slope_one": v((span, adapt), F32),
        "unit_one": v((span, width), F32),
        "inverse_one": v((span, 1), F32),
        "normed_low": v((span, width), BF16),
        "slope": v((tiles, span, width), BF16),
        "total": v((span, width), F32),
        "dffn": v((span, width), BF16),
        "dscores": v((2, span, span), BF16),
        "dvalue_t": v((LANES, span), BF16),
        "dkey_t": v((LANES, span), BF16),
        "dquery": v((span, width), BF16),
        "dkey": v((span, width), BF16),
        "dvalue": v((span, width), BF16),
    }


def layer_kernel(parts, per, lengths, tokens, cotangent, *refs):
    s = Refs()
    refs = list(refs)
    for name in INPUTS:
        setattr(s, name, refs.pop(0))
    hbm = {name: getattr(s, name) for name in BIG}
    output, grad_in, grads, vectors = (refs.pop(0) for _ in range(4))
    s.grads, s.vectors = grads, vectors
    names = list(layer_scratch(2 * LANES, 2 * LANES, 2 * LANES, 8))
    for name in names:
        setattr(s, name, refs.pop(0))
    x_in, dy_in, out_buf, grad_buf, w_sem, own_sem, send_sem, recv_sem = refs

    me = lax.axis_index("seq")
    rows = tokens.shape[1]
    mine = pl.ds(me * rows, rows)
    peers = [lax.rem(me + p, parts) for p in range(parts)]
    sources = [lax.rem(me + parts - p, parts) for p in range(parts)]

    barrier = pltpu.get_barrier_semaphore()
    for p in range(1, parts):
        pl.semaphore_signal(barrier, inc=1, device_id={"seq": peers[p]}, device_id_type=MESH)

    width = tokens.shape[2]
    weight_copies = []
    for index, name in enumerate(BIG):
        ref = getattr(s, name)
        if name == "w_inner":
            for t in range(ref.shape[0]):
                weight_copies.append(
                    pltpu.make_async_copy(hbm[name].at[:, pl.ds(t * width, width)], ref.at[t], w_sem.at[index, t])
                )
        elif name == "w_outer":
            for t in range(ref.shape[0]):
                weight_copies.append(
                    pltpu.make_async_copy(hbm[name].at[pl.ds(t * width, width), :], ref.at[t], w_sem.at[index, t])
                )
        else:
            weight_copies.append(pltpu.make_async_copy(hbm[name], ref, w_sem.at[index, 0]))
    for copy in weight_copies:
        copy.start()

    pl.semaphore_wait(barrier, parts - 1)

    def inbound(array, step, p):
        source, target = ((tokens, x_in), (cotangent, dy_in))[array]
        if p == 0:
            return pltpu.make_async_copy(
                source.at[step * parts + me], target.at[step, mine], own_sem.at[array, step]
            )
        return pltpu.make_async_remote_copy(
            src_ref=source.at[step * parts + peers[p]],
            dst_ref=target.at[step, mine],
            send_sem=send_sem.at[array, step, p],
            recv_sem=recv_sem.at[array, step, p],
            device_id={"seq": peers[p]},
            device_id_type=MESH,
        )

    def outbound(array, step, p):
        source, target = ((out_buf, output), (grad_buf, grad_in))[array - 2]
        block = source.at[step, pl.ds(peers[p] * rows, rows)]
        if p == 0:
            return pltpu.make_async_copy(block, target.at[step * parts + me], own_sem.at[array, step])
        return pltpu.make_async_remote_copy(
            src_ref=block,
            dst_ref=target.at[step * parts + me],
            send_sem=send_sem.at[array, step, p],
            recv_sem=recv_sem.at[array, step, p],
            device_id={"seq": peers[p]},
            device_id_type=MESH,
        )

    def start(make, array, step):
        for p in [*range(1, parts), 0]:
            make(array, step, p).start()

    def finish(make, array, step):
        for p in range(parts):
            make(array, step, p).wait()

    start(inbound, 0, 0)
    for ref in (grads, vectors):
        ref[...] = jnp.zeros_like(ref)
    for copy in weight_copies:
        copy.wait()

    @pl.loop(0, per)
    def _(step):
        finish(inbound, 0, step)
        start(inbound, 1, step)

        @pl.when(step + 1 < per)
        def _():
            start(inbound, 0, step + 1)

        s.output, s.grad_in = out_buf.at[step], grad_buf.at[step]
        layer(
            s,
            x_in.at[step],
            dy_in.at[step],
            lengths[step * parts + me],
            lambda: finish(inbound, 1, step),
        )
        start(outbound, 2, step)
        start(outbound, 3, step)

    @pl.loop(0, per)
    def _(step):
        finish(outbound, 2, step)
        finish(outbound, 3, step)


def per_device(parts, tokens, lengths, cotangent, *params):
    batch, rows, width = tokens.shape
    hidden, adapt = params[4].shape[1], params[6].shape[1]
    per, span = batch // parts, parts * rows
    params = [p.reshape(1, width) if p.ndim == 1 else p for p in params]
    vmem = pl.BlockSpec(memory_space=pltpu.VMEM)
    anywhere = pl.BlockSpec(memory_space=pl.ANY)
    dma = pltpu.SemaphoreType.DMA
    output, grad_in, grads, vectors = pl.pallas_call(
        functools.partial(layer_kernel, parts, per),
        out_shape=(
            jax.ShapeDtypeStruct((batch, rows, width), BF16),
            jax.ShapeDtypeStruct((batch, rows, width), BF16),
            jax.ShapeDtypeStruct((4, adapt, width), F32),
            jax.ShapeDtypeStruct((8, width), F32),
        ),
        in_specs=[pl.BlockSpec(memory_space=pltpu.SMEM)]
        + [anywhere] * 2
        + [anywhere if name in BIG else vmem for name in INPUTS],
        out_specs=(anywhere, anywhere, vmem, vmem),
        scratch_shapes=list(layer_scratch(span, width, hidden, adapt).values())
        + [pltpu.VMEM((per, span, width), BF16)] * 4
        + [dma((6, hidden // width)), dma((4, per)), dma((4, per, parts)), dma((4, per, parts))],
        compiler_params=pltpu.CompilerParams(
            collective_id=0, has_side_effects=True, vmem_limit_bytes=62 * 2**20
        ),
        name="layer",
    )(lengths, tokens, cotangent, *params)
    down_one, up_one, down_two, up_two, sums = lax.psum(
        (grads[0], grads[1], grads[2], grads[3], vectors), ("dp", "seq")
    )
    return (
        output,
        grad_in.astype(F32),
        down_one.T,
        up_one,
        down_two.T,
        up_two,
        sums[0],
        sums[1],
        sums[2],
        sums[3],
    )


def solution(mesh):
    split = P("dp", "seq", None)
    return jax.shard_map(
        functools.partial(per_device, mesh.shape["seq"]),
        mesh=mesh,
        in_specs=(split, P("dp"), split) + (P(),) * 14,
        out_specs=(split, split) + (P(),) * 8,
        check_vma=False,
    )
```

```python
import functools

import jax
import jax.numpy as jnp
from jax import lax
from jax.experimental import pallas as pl
from jax.experimental.pallas import tpu as pltpu
from jax.sharding import PartitionSpec as P

HEADS = 12
EPS = 1e-06
F32 = jnp.float32
BF16 = jnp.bfloat16
NN = (((1,), (0,)), ((), ()))
NT = (((1,), (1,)), ((), ()))
TN = (((0,), (0,)), ((), ()))
MESH = pl.DeviceIdType.MESH
LANES = 128
GROUP = 8


def dot(left, right, dims=NN):
    return lax.dot_general(left, right, dims, preferred_element_type=F32)


def gelu_parts(value):
    phi = 0.5 + 0.5 * lax.erf(value * 0.7071067811865476)
    scaled = value * jnp.exp(value * value * -0.5) * 0.3989422804014327
    return value * phi, phi + scaled


def row_mean(value):
    return jnp.sum(value, axis=-1, keepdims=True) * (1.0 / value.shape[-1])


def norm_forward(hidden):
    centred = hidden - row_mean(hidden)
    inverse = lax.rsqrt(row_mean(centred * centred) + EPS)
    return centred * inverse, inverse


def norm_backward(grad, unit, inverse, gain):
    scaled = grad * gain
    inner = scaled - row_mean(scaled) - unit * row_mean(scaled * unit)
    return inner * inverse


class Refs:
    pass


def attend_forward(s, bias):
    span = s.query.shape[1]
    half = span // 2
    low = lax.broadcasted_iota(jnp.int32, (1, LANES), 1) < LANES // 2

    @pl.loop(0, s.query.shape[0])
    def _(pair):
        key, value = s.key[pair], s.value[pair]
        zero = jnp.zeros_like(key)
        keys = (jnp.where(low, key, zero), jnp.where(low, zero, key))
        for block in range(2):
            rows = pl.ds(block * half, half)
            query = s.query[pair, rows, :]
            outs, invs = [], []
            for head in range(2):
                scores = dot(query, keys[head], NT) + bias
                top = jnp.max(scores, axis=-1, keepdims=True)
                expo = jnp.exp(scores - top)
                total = jnp.sum(expo, axis=-1, keepdims=True)
                expo_low = expo.astype(BF16)
                s.expo[2 * pair + head, rows, :] = expo_low
                outs.append(dot(expo_low, value))
                invs.append(1.0 / total)
            inv = jnp.where(low, invs[0], invs[1])
            attn = jnp.where(low, outs[0], outs[1]) * inv
            s.inv[pair, rows, :] = inv
            s.attn[pair, rows, :] = attn
            s.ctx[rows, pl.ds(pl.multiple_of(pair * LANES, LANES), LANES)] = attn.astype(BF16)


def attend_backward(s, hook=None):
    span = s.query.shape[1]
    half = span // 2
    low = lax.broadcasted_iota(jnp.int32, (1, LANES), 1) < LANES // 2

    @pl.loop(0, s.query.shape[0])
    def _(pair):
        if hook is not None:
            hook(pair)
        lanes = pl.ds(pl.multiple_of(pair * LANES, LANES), LANES)
        key, value, query = s.key[pair], s.value[pair], s.query[pair]
        zero = jnp.zeros_like(key)
        keys = (jnp.where(low, key, zero), jnp.where(low, zero, key))
        wide = s.ctx[:, lanes].astype(F32) * s.inv[pair]
        terms = wide * s.attn[pair]
        deltas = (
            jnp.sum(jnp.where(low, terms, 0.0), axis=-1, keepdims=True),
            jnp.sum(jnp.where(low, 0.0, terms), axis=-1, keepdims=True),
        )
        grad = wide.astype(BF16)
        grads = (jnp.where(low, grad, zero), jnp.where(low, zero, grad))
        grad_t, query_t = grad.T, query.T
        dquery = [None, None]
        for head in range(2):
            sub = slice(head * LANES // 2, (head + 1) * LANES // 2)
            for block in range(2):
                rows = slice(block * half, (block + 1) * half)
                expo = s.expo[2 * pair + head, pl.ds(block * half, half), :]
                dprob = dot(grads[head][rows], value, NT)
                dscores = (expo.astype(F32) * (dprob - deltas[head][rows])).astype(BF16)
                s.dscores[head, pl.ds(block * half, half), :] = dscores
                part = dot(dscores, keys[head])
                dquery[block] = part if head == 0 else dquery[block] + part
            s.dvalue_t[sub, :] = dot(grad_t[sub], s.expo[2 * pair + head]).astype(BF16)
            s.dkey_t[sub, :] = dot(query_t[sub], s.dscores[head]).astype(BF16)
        scale = (LANES // 2) ** -0.5
        for block in range(2):
            s.dquery[pl.ds(block * half, half), lanes] = (dquery[block] * scale).astype(BF16)
        s.dkey[:, lanes] = s.dkey_t[...].T
        s.dvalue[:, lanes] = s.dvalue_t[...].T


BLOCK = 256


def blocks_of(s):
    return [pl.ds(b * BLOCK, BLOCK) for b in range(s.tokens.shape[0] // BLOCK)]


def project_in(s):
    pairs = s.query.shape[0]
    scale = jnp.asarray((LANES // 2) ** -0.5, BF16)
    for rows in blocks_of(s):
        x = s.tokens[rows, :]
        for weight, target in ((s.w_query, s.query), (s.w_key, s.key), (s.w_value, s.value)):
            y = dot(x, weight[...]).astype(BF16)
            if target is s.query:
                y = y * scale
            for pair in range(pairs):
                target[pair, rows, :] = y[:, pair * LANES : (pair + 1) * LANES]


def attend_in(s):
    position = lax.broadcasted_iota(jnp.int32, (1, s.tokens.shape[0]), 1)
    attend_forward(s, jnp.where(position < s.length, 0.0, -1e30))


def first_norm(s):
    for rows in blocks_of(s):
        out = dot(s.ctx[rows, :], s.w_out[...])
        out_low = out.astype(BF16)
        s.out_low[rows, :] = out_low
        act, slope = gelu_parts(dot(out_low, s.down_one[...], NT))
        act = act.astype(BF16)
        s.act_one[rows, :] = act
        s.slope_one[rows, :] = slope
        hidden = s.tokens[rows, :].astype(F32) + out + dot(act, s.up_one[...])
        unit, inverse = norm_forward(hidden)
        s.unit_one[rows, :] = unit
        s.inverse_one[rows, :] = inverse
        normed = unit * s.gain_one[...] + s.bias_one[...]
        s.normed_low[rows, :] = normed.astype(BF16)
        s.total[rows, :] = jnp.zeros_like(normed)


def feed_forward(s):
    @pl.loop(0, s.w_inner.shape[0])
    def _(tile):
        for rows in blocks_of(s):
            act, slope = gelu_parts(dot(s.normed_low[rows, :], s.w_inner[tile]))
            s.slope[tile, rows, :] = slope.astype(BF16)
            s.total[rows, :] += dot(act.astype(BF16), s.w_outer[tile])


def second_norm(s):
    for rows in blocks_of(s):
        ffn = s.total[rows, :]
        ffn_low = ffn.astype(BF16)
        act, slope = gelu_parts(dot(ffn_low, s.down_two[...], NT))
        act = act.astype(BF16)
        normed = s.unit_one[rows, :] * s.gain_one[...] + s.bias_one[...]
        hidden = normed + ffn + dot(act, s.up_two[...])
        unit, inverse = norm_forward(hidden)
        s.output[rows, :] = (unit * s.gain_two[...] + s.bias_two[...]).astype(BF16)
        dy = s.cotangent[rows, :].astype(F32)
        s.vectors[2:3, :] += jnp.sum(dy * unit, axis=0, keepdims=True)
        s.vectors[3:4, :] += jnp.sum(dy, axis=0, keepdims=True)
        dh = norm_backward(dy, unit, inverse, s.gain_two[...])
        da = dh.astype(BF16)
        s.grads[3, :, :] += dot(act, da, TN)
        dz = (dot(da, s.up_two[...], NT) * slope).astype(BF16)
        s.grads[2, :, :] += dot(dz, ffn_low, TN)
        s.total[rows, :] = dh
        s.dffn[rows, :] = (dh + dot(dz, s.down_two[...])).astype(BF16)


def feed_backward(s):
    @pl.loop(0, s.w_inner.shape[0])
    def _(tile):
        for rows in blocks_of(s):
            du = dot(s.dffn[rows, :], s.w_outer[tile], NT) * s.slope[tile, rows, :].astype(F32)
            s.total[rows, :] += dot(du.astype(BF16), s.w_inner[tile], NT)


def first_norm_backward(s):
    for rows in blocks_of(s):
        dy = s.total[rows, :]
        unit = s.unit_one[rows, :]
        s.vectors[0:1, :] += jnp.sum(dy * unit, axis=0, keepdims=True)
        s.vectors[1:2, :] += jnp.sum(dy, axis=0, keepdims=True)
        dh = norm_backward(dy, unit, s.inverse_one[rows, :], s.gain_one[...])
        s.total[rows, :] = dh
        da = dh.astype(BF16)
        s.grads[1, :, :] += dot(s.act_one[rows, :], da, TN)
        dz = (dot(da, s.up_one[...], NT) * s.slope_one[rows, :]).astype(BF16)
        s.grads[0, :, :] += dot(dz, s.out_low[rows, :], TN)
        dout = (dh + dot(dz, s.down_one[...])).astype(BF16)
        s.ctx[rows, :] = dot(dout, s.w_out[...], NT).astype(BF16)


def project_back(s):
    for rows in blocks_of(s):
        grad = s.total[rows, :] + dot(s.dquery[rows, :], s.w_query[...], NT)
        grad = grad + dot(s.dkey[rows, :], s.w_key[...], NT)
        grad = grad + dot(s.dvalue[rows, :], s.w_value[...], NT)
        s.grad_in[rows, :] = grad.astype(BF16)


PHASES = {
    "project_in": project_in,
    "attend_in": attend_in,
    "first_norm": first_norm,
    "feed_forward": feed_forward,
    "second_norm": second_norm,
    "feed_backward": feed_backward,
    "first_norm_backward": first_norm_backward,
    "attend_backward": attend_backward,
    "project_back": project_back,
}


def small_shapes(width, adapt):
    flat = ((adapt, width), BF16)
    row = ((1, width), F32)
    return dict(zip(INPUTS[6:], (flat,) * 4 + (row,) * 4))


INPUTS = (
    "w_query", "w_key", "w_value", "w_out", "w_inner", "w_outer",
    "down_one", "up_one", "down_two", "up_two",
    "gain_one", "bias_one", "gain_two", "bias_two",
)
BIG = INPUTS[:6]


def layer_scratch(span, width, hidden, adapt):
    pairs, tiles = width // LANES, hidden // width
    v = pltpu.VMEM
    return {
        "v_w_query": v((width, width), BF16),
        "v_w_key": v((width, width), BF16),
        "v_w_value": v((width, width), BF16),
        "v_w_out": v((width, width), BF16),
        "v_w_inner": v((tiles, width, width), BF16),
        "v_w_outer": v((tiles, width, width), BF16),
        "query": v((pairs, span, LANES), BF16),
        "key": v((pairs, span, LANES), BF16),
        "value": v((pairs, span, LANES), BF16),
        "expo": v((2 * pairs, span, span), BF16),
        "inv": v((pairs, span, LANES), F32),
        "attn": v((pairs, span, LANES), F32),
        "ctx": v((span, width), BF16),
        "out_low": v((span, width), BF16),
        "act_one": v((span, adapt), BF16),
        "slope_one": v((span, adapt), F32),
        "unit_one": v((span, width), F32),
        "inverse_one": v((span, 1), F32),
        "normed_low": v((span, width), BF16),
        "slope": v((tiles, span, width), BF16),
        "total": v((span, width), F32),
        "dffn": v((span, width), BF16),
        "dscores": v((2, span, span), BF16),
        "dvalue_t": v((LANES, span), BF16),
        "dkey_t": v((LANES, span), BF16),
        "dquery": v((span, width), BF16),
        "dkey": v((span, width), BF16),
        "dvalue": v((span, width), BF16),
    }


class Reduce:
    def __init__(self, s, parts, devices, me, refs):
        self.s, self.parts, self.me = s, parts, me
        self.outer = devices // GROUP
        self.place = lax.axis_index("dp")
        self.inner = lax.rem(self.place, GROUP)
        self.base = self.place - self.inner
        self.send, self.got_seq, self.part, self.got_dp, self.got_outer, self.full, self.sems = refs

    def seq_peer(self, p):
        return lax.rem(self.me + p, self.parts)

    def inner_peer(self, k):
        return lax.rem(self.inner + k, GROUP)

    def dp_peer(self, k):
        return self.base + self.inner_peer(k)

    def outer_peer(self, k):
        return lax.rem(self.place + k * GROUP, self.outer * GROUP)

    def greeted(self):
        return (
            [{"seq": self.seq_peer(p)} for p in range(1, self.parts)]
            + [{"dp": self.dp_peer(k)} for k in range(1, GROUP)]
            + [{"dp": self.outer_peer(k)} for k in range(1, self.outer)]
        )

    def copy(self, stage, k, source, target, device):
        return pltpu.make_async_remote_copy(
            src_ref=source,
            dst_ref=target,
            send_sem=self.sems.at[0, stage, k],
            recv_sem=self.sems.at[1, stage, k],
            device_id=device,
            device_id_type=MESH,
        )

    def copies(self, stage):
        mine = self.me * GROUP
        if stage == 0:
            return [
                self.copy(
                    0, p, self.send.at[pl.ds(self.seq_peer(p) * GROUP, GROUP)], self.got_seq.at[p], {"seq": self.seq_peer(p)}
                )
                for p in range(1, self.parts)
            ]
        if stage == 1:
            return [
                self.copy(1, k, self.part.at[self.inner_peer(k)], self.got_dp.at[k], {"dp": self.dp_peer(k)})
                for k in range(1, GROUP)
            ]
        if stage == 2:
            return [
                self.copy(2, k, self.got_outer.at[0], self.got_outer.at[k], {"dp": self.outer_peer(k)})
                for k in range(1, self.outer)
            ]
        if stage == 3:
            block = self.full.at[mine + self.inner]
            return [self.copy(3, k, block, block, {"dp": self.dp_peer(k)}) for k in range(1, GROUP)]
        block = self.full.at[pl.ds(mine, GROUP)]
        return [self.copy(4, p, block, block, {"seq": self.seq_peer(p)}) for p in range(1, self.parts)]

    def start(self, stage):
        for copy in self.copies(stage):
            copy.start()

    def finish(self, stage):
        for copy in self.copies(stage):
            copy.wait()

    def first(self):
        grads, vectors = self.s.grads, self.s.vectors
        adapt, width = grads.shape[1:]
        chunks, rows = self.send.shape[:2]
        head = lax.broadcasted_iota(jnp.int32, (rows, LANES), 0) == 0
        pairs = width // LANES
        for c in range(chunks):
            first = c * rows
            self.send[c, :, :width] = grads[first // adapt, first % adapt : first % adapt + rows, :].astype(BF16)
            tail = jnp.zeros((rows, LANES), F32)
            if c < 4 * pairs:
                vector = vectors[c // pairs : c // pairs + 1, (c % pairs) * LANES : (c % pairs + 1) * LANES]
                tail = jnp.where(head, vector, tail)
            self.send[c, :, width:] = tail.astype(BF16)
        self.start(0)

    def second(self):
        self.finish(0)
        total = self.send[pl.ds(self.me * GROUP, GROUP)].astype(F32)
        for p in range(1, self.parts):
            total = total + self.got_seq[p].astype(F32)
        self.part[...] = total.astype(BF16)
        self.start(1)

    def third(self):
        self.finish(1)
        total = self.part[self.inner].astype(F32)
        for k in range(1, GROUP):
            total = total + self.got_dp[k].astype(F32)
        if self.outer > 1:
            self.got_outer[0] = total.astype(BF16)
            self.start(2)
            self.finish(2)
            group = self.place // GROUP
            total = jnp.zeros_like(total)
            for a in range(self.outer):
                total = total + self.got_outer[lax.rem(group + self.outer - a, self.outer)].astype(F32)
        self.full[self.me * GROUP + self.inner] = total.astype(BF16)
        self.start(3)

    def fourth(self):
        self.finish(3)
        self.start(4)

    def last(self, grads, vectors):
        self.finish(4)
        adapt, width = self.s.grads.shape[1:]
        chunks, rows = self.send.shape[:2]
        pairs = width // LANES
        for c in range(chunks):
            first = c * rows
            chunk = self.full[c].astype(F32)
            grads[first // adapt][first % adapt : first % adapt + rows, :] = chunk[:, :width]
            if c < 4 * pairs:
                lanes = slice((c % pairs) * LANES, (c % pairs + 1) * LANES)
                vectors[c // pairs][lanes] = chunk[0, width:]


def layer_kernel(parts, devices, per, lengths, tokens, cotangent, *refs):
    s = Refs()
    refs = list(refs)
    for name in INPUTS:
        setattr(s, name, refs.pop(0))
    for name in INPUTS[10:]:
        setattr(s, name, getattr(s, name)[...].reshape(1, -1))
    hbm = {name: getattr(s, name) for name in BIG}
    output, grad_in = refs.pop(0), refs.pop(0)
    grads_out = [refs.pop(0) for _ in range(4)]
    vectors_out = [refs.pop(0) for _ in range(4)]
    for name in layer_scratch(LANES, LANES, LANES, 8):
        setattr(s, name, refs.pop(0))
    s.grads, s.vectors, x_in, dy_in, out_buf, grad_buf = (refs.pop(0) for _ in range(6))
    w_sem, own_sem, send_sem, recv_sem = (refs.pop(0) for _ in range(4))

    me = lax.axis_index("seq")
    rows = tokens.shape[1]
    mine = pl.ds(me * rows, rows)
    peers = [lax.rem(me + p, parts) for p in range(parts)]
    reduce = Reduce(s, parts, devices, me, refs)

    barrier = pltpu.get_barrier_semaphore()
    for device in reduce.greeted():
        pl.semaphore_signal(barrier, inc=1, device_id=device, device_id_type=MESH)

    width = tokens.shape[2]
    weight_copies = []
    for index, name in enumerate(BIG):
        ref = getattr(s, "v_" + name)
        if name == "w_inner":
            for t in range(ref.shape[0]):
                weight_copies.append(
                    pltpu.make_async_copy(hbm[name].at[:, pl.ds(t * width, width)], ref.at[t], w_sem.at[index, t])
                )
        elif name == "w_outer":
            for t in range(ref.shape[0]):
                weight_copies.append(
                    pltpu.make_async_copy(hbm[name].at[pl.ds(t * width, width), :], ref.at[t], w_sem.at[index, t])
                )
        else:
            weight_copies.append(pltpu.make_async_copy(hbm[name], ref, w_sem.at[index, 0]))
        setattr(s, name, ref)

    pl.semaphore_wait(barrier, len(reduce.greeted()))

    def copies(array, step):
        made = []
        for p in [*range(1, parts), 0]:
            if array < 2:
                source, target = ((tokens, x_in), (cotangent, dy_in))[array]
                source, target = source.at[step * parts + peers[p]], target.at[step, mine]
            else:
                source, target = ((out_buf, output), (grad_buf, grad_in))[array - 2]
                source, target = source.at[step, pl.ds(peers[p] * rows, rows)], target.at[step * parts + me]
            if p == 0:
                made.append(pltpu.make_async_copy(source, target, own_sem.at[array, step]))
            else:
                made.append(
                    pltpu.make_async_remote_copy(
                        src_ref=source,
                        dst_ref=target,
                        send_sem=send_sem.at[array, step, p],
                        recv_sem=recv_sem.at[array, step, p],
                        device_id={"seq": peers[p]},
                        device_id_type=MESH,
                    )
                )
        return made

    def start(array, step):
        for copy in copies(array, step):
            copy.start()

    def finish(array, step):
        for copy in copies(array, step):
            copy.wait()

    start(0, 0)
    for copy in weight_copies:
        copy.start()
    for ref in (s.grads, s.vectors):
        ref[...] = jnp.zeros_like(ref)
    for copy in weight_copies:
        copy.wait()

    @pl.loop(0, per)
    def _(step):
        more, final = step + 1 < per, step == per - 1
        s.tokens, s.cotangent = x_in.at[step], dy_in.at[step]
        s.output, s.grad_in = out_buf.at[step], grad_buf.at[step]
        s.length = lengths[step * parts + me]
        finish(0, step)

        @pl.when(step == 0)
        def _():
            start(1, 0)

        @pl.when(more)
        def _():
            start(0, step + 1)

        project_in(s)
        attend_in(s)
        first_norm(s)
        feed_forward(s)
        finish(1, step)

        @pl.when(more)
        def _():
            start(1, step + 1)

        second_norm(s)
        start(2, step)
        feed_backward(s)
        first_norm_backward(s)

        @pl.when(final)
        def _():
            reduce.first()

        def hook(pair):
            for at, stage in ((1, reduce.second), (3, reduce.third), (5, reduce.fourth)):
                pl.when(final & (pair == at))(stage)

        attend_backward(s, hook)
        project_back(s)
        start(3, step)

    reduce.last(grads_out, vectors_out)

    @pl.loop(0, per)
    def _(step):
        finish(2, step)
        finish(3, step)


def per_device(parts, devices, tokens, lengths, cotangent, *params):
    batch, rows, width = tokens.shape
    hidden, adapt = params[4].shape[1], params[6].shape[1]
    per, span = batch // parts, parts * rows
    chunks, chunk_rows = parts * GROUP, 4 * adapt // (parts * GROUP)
    outer = devices // GROUP
    params = list(params)
    params[6], params[8] = params[6].T, params[8].T
    vmem = pl.BlockSpec(memory_space=pltpu.VMEM)
    anywhere = pl.BlockSpec(memory_space=pl.ANY)
    dma = pltpu.SemaphoreType.DMA
    scratch = [
        *layer_scratch(span, width, hidden, adapt).values(),
        pltpu.VMEM((4, adapt, width), F32),
        pltpu.VMEM((8, width), F32),
        *[pltpu.VMEM((per, span, width), BF16)] * 4,
        dma((len(BIG), hidden // width)),
        dma((4, per)),
        dma((4, per, parts)),
        dma((4, per, parts)),
    ]
    chunk = (chunk_rows, width + LANES)
    scratch += [
        pltpu.VMEM((chunks, *chunk), BF16),
        pltpu.VMEM((parts, GROUP, *chunk), BF16),
        pltpu.VMEM((GROUP, *chunk), BF16),
        pltpu.VMEM((GROUP, *chunk), BF16),
        pltpu.VMEM((outer, *chunk), BF16),
        pltpu.VMEM((chunks, *chunk), BF16),
        dma((2, 5, max(parts, GROUP, outer))),
    ]
    results = pl.pallas_call(
        functools.partial(layer_kernel, parts, devices, per),
        out_shape=(jax.ShapeDtypeStruct((batch, rows, width), BF16),) * 2
        + (jax.ShapeDtypeStruct((adapt, width), F32),) * 4
        + (jax.ShapeDtypeStruct((width,), F32),) * 4,
        in_specs=[pl.BlockSpec(memory_space=pltpu.SMEM)]
        + [anywhere] * 2
        + [anywhere if name in BIG else vmem for name in INPUTS],
        out_specs=(anywhere,) * 2 + (vmem,) * 8,
        scratch_shapes=scratch,
        compiler_params=pltpu.CompilerParams(
            collective_id=0, has_side_effects=True, vmem_limit_bytes=62 * 2**20
        ),
        name="layer",
    )(lengths, tokens, cotangent, *params)
    output, grad_in, down_one, up_one, down_two, up_two, *vectors = results
    return (output, grad_in.astype(F32), down_one.T, up_one, down_two.T, up_two, *vectors)


def solution(mesh):
    split = P("dp", "seq", None)
    return jax.shard_map(
        functools.partial(per_device, mesh.shape["seq"], mesh.shape["dp"]),
        mesh=mesh,
        in_specs=(split, P("dp"), split) + (P(),) * 14,
        out_specs=(split, split) + (P(),) * 8,
        check_vma=False,
    )
```

```python
import functools

import jax
import jax.numpy as jnp
from jax import lax
from jax.experimental import pallas as pl
from jax.experimental.pallas import tpu as pltpu
from jax.sharding import PartitionSpec as P

HEADS = 12
EPS = 1e-06
F32 = jnp.float32
BF16 = jnp.bfloat16
NN = (((1,), (0,)), ((), ()))
NT = (((1,), (1,)), ((), ()))
TN = (((0,), (0,)), ((), ()))
MESH = pl.DeviceIdType.MESH
LANES = 128
GROUP = 8


def dot(left, right, dims=NN):
    return lax.dot_general(left, right, dims, preferred_element_type=F32)


def gelu_parts(value):
    phi = 0.5 + 0.5 * lax.erf(value * 0.7071067811865476)
    scaled = value * jnp.exp(value * value * -0.5) * 0.3989422804014327
    return value * phi, phi + scaled


def row_mean(value):
    return jnp.sum(value, axis=-1, keepdims=True) * (1.0 / value.shape[-1])


def norm_forward(hidden):
    centred = hidden - row_mean(hidden)
    inverse = lax.rsqrt(row_mean(centred * centred) + EPS)
    return centred * inverse, inverse


def norm_backward(grad, unit, inverse, gain):
    scaled = grad * gain
    inner = scaled - row_mean(scaled) - unit * row_mean(scaled * unit)
    return inner * inverse


class Refs:
    pass


def pair_lanes(pair):
    return slice(pair * LANES, (pair + 1) * LANES)


def attend_forward(s):
    pairs, span = s.query.shape[:2]
    low = lax.broadcasted_iota(jnp.int32, (1, LANES), 1) < LANES // 2
    bias = jnp.where(lax.broadcasted_iota(jnp.int32, (1, span), 1) < s.length, 0.0, -1e30)
    for pair in range(pairs):
        key, value = s.key[pair], s.value[pair]
        zero = jnp.zeros_like(key)
        keys = (jnp.where(low, key, zero), jnp.where(low, zero, key))
        value = jnp.concatenate([value, jnp.ones_like(value)], axis=1)
        for rows in blocks_of(s):
            query = s.query[pair, rows, :]
            outs, totals = [], []
            for head in range(2):
                scores = dot(query, keys[head], NT) + bias
                expo = jnp.exp(scores - jnp.max(scores, axis=-1, keepdims=True)).astype(BF16)
                s.expo[2 * pair + head, rows, :] = expo
                product = dot(expo, value)
                outs.append(product[:, :LANES])
                totals.append(product[:, LANES:])
            inv = 1.0 / jnp.where(low, *totals)
            attn = jnp.where(low, *outs) * inv
            s.inv[pair, rows, :] = inv
            s.attn[pair, rows, :] = attn
            s.ctx[rows, pair_lanes(pair)] = attn.astype(BF16)


def attend_backward(s, pair):
    low = lax.broadcasted_iota(jnp.int32, (1, LANES), 1) < LANES // 2
    lanes = pair_lanes(pair)
    key, value, query = s.key[pair], s.value[pair], s.query[pair]
    zero = jnp.zeros_like(key)
    wide = s.ctx[:, lanes].astype(F32) * s.inv[pair]
    terms = wide * s.attn[pair]
    grad = wide.astype(BF16)
    grad_t, query_t = grad.T, query.T
    dquery, dkey, dvalue = 0.0, [], []
    for head in range(2):
        mine = low if head == 0 else ~low
        sub = slice(head * LANES // 2, (head + 1) * LANES // 2)
        delta = jnp.sum(jnp.where(mine, terms, 0.0), axis=-1, keepdims=True)
        expo = s.expo[2 * pair + head]
        dprob = dot(jnp.where(mine, grad, zero), value, NT)
        dscores = (expo.astype(F32) * (dprob - delta)).astype(BF16)
        dquery = dquery + dot(dscores, jnp.where(mine, key, zero))
        dvalue.append(dot(grad_t[sub], expo).astype(BF16))
        dkey.append(dot(query_t[sub], dscores).astype(BF16))
    s.dquery[:, lanes] = (dquery * (LANES // 2) ** -0.5).astype(BF16)
    s.dkey[:, lanes] = jnp.concatenate(dkey, axis=0).T
    s.dvalue[:, lanes] = jnp.concatenate(dvalue, axis=0).T


BLOCK = 256


def blocks_of(s):
    return [pl.ds(b * BLOCK, BLOCK) for b in range(s.tokens.shape[0] // BLOCK)]


def project_in(s):
    pairs = s.query.shape[0]
    scale = jnp.asarray((LANES // 2) ** -0.5, BF16)
    for rows in blocks_of(s):
        x = s.tokens[rows, :]
        for weight, target in ((s.w_query, s.query), (s.w_key, s.key), (s.w_value, s.value)):
            y = dot(x, weight[...]).astype(BF16)
            if target is s.query:
                y = y * scale
            for pair in range(pairs):
                target[pair, rows, :] = y[:, pair * LANES : (pair + 1) * LANES]


def first_norm(s):
    for rows in blocks_of(s):
        out = dot(s.ctx[rows, :], s.w_out[...])
        out_low = out.astype(BF16)
        s.out_low[rows, :] = out_low
        act, slope = gelu_parts(dot(out_low, s.down_one[...], NT))
        act = act.astype(BF16)
        s.act_one[rows, :] = act
        s.slope_one[rows, :] = slope
        hidden = s.tokens[rows, :].astype(F32) + out + dot(act, s.up_one[...])
        unit, inverse = norm_forward(hidden)
        s.unit_one[rows, :] = unit
        s.inverse_one[rows, :] = inverse
        normed = unit * s.gain_one[...] + s.bias_one[...]
        s.normed_low[rows, :] = normed.astype(BF16)
        s.total[rows, :] = jnp.zeros_like(normed)


def feed_forward(s):
    for tile in range(s.w_inner.shape[0]):
        for rows in blocks_of(s):
            act, slope = gelu_parts(dot(s.normed_low[rows, :], s.w_inner[tile]))
            s.slope[tile, rows, :] = slope.astype(BF16)
            s.total[rows, :] += dot(act.astype(BF16), s.w_outer[tile])


def second_norm(s):
    for rows in blocks_of(s):
        ffn = s.total[rows, :]
        ffn_low = ffn.astype(BF16)
        act, slope = gelu_parts(dot(ffn_low, s.down_two[...], NT))
        act = act.astype(BF16)
        normed = s.unit_one[rows, :] * s.gain_one[...] + s.bias_one[...]
        hidden = normed + ffn + dot(act, s.up_two[...])
        unit, inverse = norm_forward(hidden)
        s.output[rows, :] = (unit * s.gain_two[...] + s.bias_two[...]).astype(BF16)
        dy = s.cotangent[rows, :].astype(F32)
        s.vectors[2:3, :] += jnp.sum(dy * unit, axis=0, keepdims=True)
        s.vectors[3:4, :] += jnp.sum(dy, axis=0, keepdims=True)
        dh = norm_backward(dy, unit, inverse, s.gain_two[...])
        da = dh.astype(BF16)
        s.grads[3, :, :] += dot(act, da, TN)
        dz = (dot(da, s.up_two[...], NT) * slope).astype(BF16)
        s.grads[2, :, :] += dot(dz, ffn_low, TN)
        s.total[rows, :] = dh
        s.dffn[rows, :] = (dh + dot(dz, s.down_two[...])).astype(BF16)


def feed_backward(s):
    for tile in range(s.w_inner.shape[0]):
        for rows in blocks_of(s):
            du = dot(s.dffn[rows, :], s.w_outer[tile], NT) * s.slope[tile, rows, :].astype(F32)
            s.total[rows, :] += dot(du.astype(BF16), s.w_inner[tile], NT)


def first_norm_backward(s):
    for rows in blocks_of(s):
        dy = s.total[rows, :]
        unit = s.unit_one[rows, :]
        s.vectors[0:1, :] += jnp.sum(dy * unit, axis=0, keepdims=True)
        s.vectors[1:2, :] += jnp.sum(dy, axis=0, keepdims=True)
        dh = norm_backward(dy, unit, s.inverse_one[rows, :], s.gain_one[...])
        s.total[rows, :] = dh
        da = dh.astype(BF16)
        s.grads[1, :, :] += dot(s.act_one[rows, :], da, TN)
        dz = (dot(da, s.up_one[...], NT) * s.slope_one[rows, :]).astype(BF16)
        s.grads[0, :, :] += dot(dz, s.out_low[rows, :], TN)
        dout = (dh + dot(dz, s.down_one[...])).astype(BF16)
        s.ctx[rows, :] = dot(dout, s.w_out[...], NT).astype(BF16)


def project_back(s):
    for rows in blocks_of(s):
        grad = s.total[rows, :] + dot(s.dquery[rows, :], s.w_query[...], NT)
        grad = grad + dot(s.dkey[rows, :], s.w_key[...], NT)
        grad = grad + dot(s.dvalue[rows, :], s.w_value[...], NT)
        s.grad_in[rows, :] = grad.astype(BF16)


PHASES = {
    "project_in": project_in,
    "attend_forward": attend_forward,
    "first_norm": first_norm,
    "feed_forward": feed_forward,
    "second_norm": second_norm,
    "feed_backward": feed_backward,
    "first_norm_backward": first_norm_backward,
    "attend_backward": lambda s: [attend_backward(s, pair) for pair in range(6)],
    "project_back": project_back,
}


def small_shapes(width, adapt):
    flat = ((adapt, width), BF16)
    row = ((1, width), F32)
    return dict(zip(INPUTS[6:], (flat,) * 4 + (row,) * 4))


INPUTS = (
    "w_query", "w_key", "w_value", "w_out", "w_inner", "w_outer",
    "down_one", "up_one", "down_two", "up_two",
    "gain_one", "bias_one", "gain_two", "bias_two",
)
BIG = INPUTS[:6]


def layer_scratch(span, width, hidden, adapt):
    pairs, tiles = width // LANES, hidden // width
    v = pltpu.VMEM
    return {
        "v_w_query": v((width, width), BF16),
        "v_w_key": v((width, width), BF16),
        "v_w_value": v((width, width), BF16),
        "v_w_out": v((width, width), BF16),
        "v_w_inner": v((tiles, width, width), BF16),
        "v_w_outer": v((tiles, width, width), BF16),
        "query": v((pairs, span, LANES), BF16),
        "key": v((pairs, span, LANES), BF16),
        "value": v((pairs, span, LANES), BF16),
        "expo": v((2 * pairs, span, span), BF16),
        "inv": v((pairs, span, LANES), F32),
        "attn": v((pairs, span, LANES), F32),
        "ctx": v((span, width), BF16),
        "out_low": v((span, width), BF16),
        "act_one": v((span, adapt), BF16),
        "slope_one": v((span, adapt), F32),
        "unit_one": v((span, width), F32),
        "inverse_one": v((span, 1), F32),
        "normed_low": v((span, width), BF16),
        "slope": v((tiles, span, width), BF16),
        "total": v((span, width), F32),
        "dffn": v((span, width), BF16),
        "dquery": v((span, width), BF16),
        "dkey": v((span, width), BF16),
        "dvalue": v((span, width), BF16),
    }


class Reduce:
    def __init__(self, s, parts, devices, me, refs):
        self.s, self.parts, self.me = s, parts, me
        self.outer = devices // GROUP
        self.place = lax.axis_index("dp")
        self.inner = lax.rem(self.place, GROUP)
        self.base = self.place - self.inner
        self.send, self.got_seq, self.part, self.got_dp, self.got_outer, self.full, self.sems = refs

    def seq_peer(self, p):
        return lax.rem(self.me + p, self.parts)

    def inner_peer(self, k):
        return lax.rem(self.inner + k, GROUP)

    def dp_peer(self, k):
        return self.base + self.inner_peer(k)

    def outer_peer(self, k):
        return lax.rem(self.place + k * GROUP, self.outer * GROUP)

    def greeted(self):
        return (
            [{"seq": self.seq_peer(p)} for p in range(1, self.parts)]
            + [{"dp": self.dp_peer(k)} for k in range(1, GROUP)]
            + [{"dp": self.outer_peer(k)} for k in range(1, self.outer)]
        )

    def copy(self, stage, k, source, target, device):
        return pltpu.make_async_remote_copy(
            src_ref=source,
            dst_ref=target,
            send_sem=self.sems.at[0, stage, k],
            recv_sem=self.sems.at[1, stage, k],
            device_id=device,
            device_id_type=MESH,
        )

    def copies(self, stage):
        mine = self.me * GROUP
        if stage == 0:
            return [
                self.copy(
                    0, p, self.send.at[pl.ds(self.seq_peer(p) * GROUP, GROUP)], self.got_seq.at[p], {"seq": self.seq_peer(p)}
                )
                for p in range(1, self.parts)
            ]
        if stage == 1:
            return [
                self.copy(1, k, self.part.at[self.inner_peer(k)], self.got_dp.at[k], {"dp": self.dp_peer(k)})
                for k in range(1, GROUP)
            ]
        if stage == 2:
            return [
                self.copy(2, k, self.got_outer.at[0], self.got_outer.at[k], {"dp": self.outer_peer(k)})
                for k in range(1, self.outer)
            ]
        if stage == 3:
            block = self.full.at[mine + self.inner]
            return [self.copy(3, k, block, block, {"dp": self.dp_peer(k)}) for k in range(1, GROUP)]
        block = self.full.at[pl.ds(mine, GROUP)]
        return [self.copy(4, p, block, block, {"seq": self.seq_peer(p)}) for p in range(1, self.parts)]

    def start(self, stage):
        for copy in self.copies(stage):
            copy.start()

    def finish(self, stage):
        for copy in self.copies(stage):
            copy.wait()

    def first(self):
        grads, vectors = self.s.grads, self.s.vectors
        adapt, width = grads.shape[1:]
        chunks, rows = self.send.shape[:2]
        head = lax.broadcasted_iota(jnp.int32, (rows, LANES), 0) == 0
        pairs = width // LANES
        for c in range(chunks):
            first = c * rows
            self.send[c, :, :width] = grads[first // adapt, first % adapt : first % adapt + rows, :].astype(BF16)
            tail = jnp.zeros((rows, LANES), F32)
            if c < 4 * pairs:
                vector = vectors[c // pairs : c // pairs + 1, (c % pairs) * LANES : (c % pairs + 1) * LANES]
                tail = jnp.where(head, vector, tail)
            self.send[c, :, width:] = tail.astype(BF16)
        self.start(0)

    def second(self):
        self.finish(0)
        total = self.send[pl.ds(self.me * GROUP, GROUP)].astype(F32)
        for p in range(1, self.parts):
            total = total + self.got_seq[p].astype(F32)
        self.part[...] = total.astype(BF16)
        self.start(1)

    def third(self):
        self.finish(1)
        total = self.part[self.inner].astype(F32)
        for k in range(1, GROUP):
            total = total + self.got_dp[k].astype(F32)
        if self.outer > 1:
            self.got_outer[0] = total.astype(BF16)
            self.start(2)
            self.finish(2)
            group = self.place // GROUP
            total = jnp.zeros_like(total)
            for a in range(self.outer):
                total = total + self.got_outer[lax.rem(group + self.outer - a, self.outer)].astype(F32)
        self.full[self.me * GROUP + self.inner] = total.astype(BF16)
        self.start(3)

    def fourth(self):
        self.finish(3)
        self.start(4)

    def last(self, grads, vectors):
        self.finish(4)
        adapt, width = self.s.grads.shape[1:]
        chunks, rows = self.send.shape[:2]
        pairs = width // LANES
        for c in range(chunks):
            first = c * rows
            chunk = self.full[c].astype(F32)
            grads[first // adapt][first % adapt : first % adapt + rows, :] = chunk[:, :width]
            if c < 4 * pairs:
                lanes = slice((c % pairs) * LANES, (c % pairs + 1) * LANES)
                vectors[c // pairs][lanes] = chunk[0, width:]


def layer_kernel(parts, devices, per, lengths, tokens, cotangent, *refs):
    s = Refs()
    refs = list(refs)
    for name in INPUTS:
        setattr(s, name, refs.pop(0))
    for name in INPUTS[10:]:
        setattr(s, name, getattr(s, name)[...].reshape(1, -1))
    hbm = {name: getattr(s, name) for name in BIG}
    output, grad_in = refs.pop(0), refs.pop(0)
    grads_out = [refs.pop(0) for _ in range(4)]
    vectors_out = [refs.pop(0) for _ in range(4)]
    for name in layer_scratch(LANES, LANES, LANES, 8):
        setattr(s, name, refs.pop(0))
    s.grads, s.vectors, x_in, dy_in, out_buf, grad_buf = (refs.pop(0) for _ in range(6))
    w_sem, own_sem, send_sem, recv_sem = (refs.pop(0) for _ in range(4))

    me = lax.axis_index("seq")
    rows = tokens.shape[1]
    mine = pl.ds(me * rows, rows)
    peers = [lax.rem(me + p, parts) for p in range(parts)]
    reduce = Reduce(s, parts, devices, me, refs)

    barrier = pltpu.get_barrier_semaphore()
    for device in reduce.greeted():
        pl.semaphore_signal(barrier, inc=1, device_id=device, device_id_type=MESH)

    width = tokens.shape[2]
    weight_copies = []
    for index, name in enumerate(BIG):
        ref = getattr(s, "v_" + name)
        if name == "w_inner":
            for t in range(ref.shape[0]):
                weight_copies.append(
                    pltpu.make_async_copy(hbm[name].at[:, pl.ds(t * width, width)], ref.at[t], w_sem.at[index, t])
                )
        elif name == "w_outer":
            for t in range(ref.shape[0]):
                weight_copies.append(
                    pltpu.make_async_copy(hbm[name].at[pl.ds(t * width, width), :], ref.at[t], w_sem.at[index, t])
                )
        else:
            weight_copies.append(pltpu.make_async_copy(hbm[name], ref, w_sem.at[index, 0]))
        setattr(s, name, ref)

    pl.semaphore_wait(barrier, len(reduce.greeted()))

    def copies(array, step):
        made = []
        for p in [*range(1, parts), 0]:
            if array < 2:
                source, target = ((tokens, x_in), (cotangent, dy_in))[array]
                source, target = source.at[step * parts + peers[p]], target.at[step, mine]
            else:
                source, target = ((out_buf, output), (grad_buf, grad_in))[array - 2]
                source, target = source.at[step, pl.ds(peers[p] * rows, rows)], target.at[step * parts + me]
            if p == 0:
                made.append(pltpu.make_async_copy(source, target, own_sem.at[array, step]))
            else:
                made.append(
                    pltpu.make_async_remote_copy(
                        src_ref=source,
                        dst_ref=target,
                        send_sem=send_sem.at[array, step, p],
                        recv_sem=recv_sem.at[array, step, p],
                        device_id={"seq": peers[p]},
                        device_id_type=MESH,
                    )
                )
        return made

    def start(array, step):
        for copy in copies(array, step):
            copy.start()

    def finish(array, step):
        for copy in copies(array, step):
            copy.wait()

    start(0, 0)
    for copy in weight_copies:
        copy.start()
    for ref in (s.grads, s.vectors):
        ref[...] = jnp.zeros_like(ref)
    for copy in weight_copies:
        copy.wait()

    @pl.loop(0, per)
    def _(step):
        more, final = step + 1 < per, step == per - 1
        s.tokens, s.cotangent = x_in.at[step], dy_in.at[step]
        s.output, s.grad_in = out_buf.at[step], grad_buf.at[step]
        s.length = lengths[step * parts + me]
        finish(0, step)

        @pl.when(step == 0)
        def _():
            start(1, 0)

        @pl.when(more)
        def _():
            start(0, step + 1)

        project_in(s)
        attend_forward(s)
        first_norm(s)
        feed_forward(s)
        finish(1, step)

        @pl.when(more)
        def _():
            start(1, step + 1)

        second_norm(s)
        start(2, step)
        feed_backward(s)
        first_norm_backward(s)

        @pl.when(final)
        def _():
            reduce.first()

        stages = {1: reduce.second, 3: reduce.third, 5: reduce.fourth}
        for pair in range(s.query.shape[0]):
            attend_backward(s, pair)
            if pair in stages:
                pl.when(final)(stages[pair])
        project_back(s)
        start(3, step)

    reduce.last(grads_out, vectors_out)

    @pl.loop(0, per)
    def _(step):
        finish(2, step)
        finish(3, step)


def per_device(parts, devices, tokens, lengths, cotangent, *params):
    batch, rows, width = tokens.shape
    hidden, adapt = params[4].shape[1], params[6].shape[1]
    per, span = batch // parts, parts * rows
    chunks, chunk_rows = parts * GROUP, 4 * adapt // (parts * GROUP)
    outer = devices // GROUP
    params = list(params)
    params[6], params[8] = params[6].T, params[8].T
    vmem = pl.BlockSpec(memory_space=pltpu.VMEM)
    anywhere = pl.BlockSpec(memory_space=pl.ANY)
    dma = pltpu.SemaphoreType.DMA
    scratch = [
        *layer_scratch(span, width, hidden, adapt).values(),
        pltpu.VMEM((4, adapt, width), F32),
        pltpu.VMEM((8, width), F32),
        *[pltpu.VMEM((per, span, width), BF16)] * 4,
        dma((len(BIG), hidden // width)),
        dma((4, per)),
        dma((4, per, parts)),
        dma((4, per, parts)),
    ]
    chunk = (chunk_rows, width + LANES)
    scratch += [
        pltpu.VMEM((chunks, *chunk), BF16),
        pltpu.VMEM((parts, GROUP, *chunk), BF16),
        pltpu.VMEM((GROUP, *chunk), BF16),
        pltpu.VMEM((GROUP, *chunk), BF16),
        pltpu.VMEM((outer, *chunk), BF16),
        pltpu.VMEM((chunks, *chunk), BF16),
        dma((2, 5, max(parts, GROUP, outer))),
    ]
    results = pl.pallas_call(
        functools.partial(layer_kernel, parts, devices, per),
        out_shape=(jax.ShapeDtypeStruct((batch, rows, width), BF16),) * 2
        + (jax.ShapeDtypeStruct((adapt, width), F32),) * 4
        + (jax.ShapeDtypeStruct((width,), F32),) * 4,
        in_specs=[pl.BlockSpec(memory_space=pltpu.SMEM)]
        + [anywhere] * 2
        + [anywhere if name in BIG else vmem for name in INPUTS],
        out_specs=(anywhere,) * 2 + (vmem,) * 8,
        scratch_shapes=scratch,
        compiler_params=pltpu.CompilerParams(
            collective_id=0, has_side_effects=True, vmem_limit_bytes=62 * 2**20
        ),
        name="layer",
    )(lengths, tokens, cotangent, *params)
    output, grad_in, down_one, up_one, down_two, up_two, *vectors = results
    return (output, grad_in.astype(F32), down_one.T, up_one, down_two.T, up_two, *vectors)


def solution(mesh):
    split = P("dp", "seq", None)
    return jax.shard_map(
        functools.partial(per_device, mesh.shape["seq"], mesh.shape["dp"]),
        mesh=mesh,
        in_specs=(split, P("dp"), split) + (P(),) * 14,
        out_specs=(split, split) + (P(),) * 8,
        check_vma=False,
    )
```

```python
import functools

import jax
import jax.numpy as jnp
from jax import lax
from jax.experimental import pallas as pl
from jax.experimental.pallas import tpu as pltpu
from jax.sharding import PartitionSpec as P

HEADS = 12
EPS = 1e-06
F32 = jnp.float32
BF16 = jnp.bfloat16
NN = (((1,), (0,)), ((), ()))
NT = (((1,), (1,)), ((), ()))
TN = (((0,), (0,)), ((), ()))
MESH = pl.DeviceIdType.MESH
LANES = 128
GROUP = 8


def dot(left, right, dims=NN):
    return lax.dot_general(left, right, dims, preferred_element_type=F32)


def gelu_parts(value):
    phi = 0.5 + 0.5 * lax.erf(value * 0.7071067811865476)
    scaled = value * jnp.exp(value * value * -0.5) * 0.3989422804014327
    return value * phi, phi + scaled


def row_mean(value):
    return jnp.sum(value, axis=-1, keepdims=True) * (1.0 / value.shape[-1])


def norm_forward(hidden):
    centred = hidden - row_mean(hidden)
    inverse = lax.rsqrt(row_mean(centred * centred) + EPS)
    return centred * inverse, inverse


def norm_backward(grad, unit, inverse, gain):
    scaled = grad * gain
    inner = scaled - row_mean(scaled) - unit * row_mean(scaled * unit)
    return inner * inverse


class Refs:
    pass


def pair_lanes(pair):
    return slice(pair * LANES, (pair + 1) * LANES)


def attend_forward(s):
    pairs, span = s.query.shape[:2]
    low = lax.broadcasted_iota(jnp.int32, (1, LANES), 1) < LANES // 2
    bias = jnp.where(lax.broadcasted_iota(jnp.int32, (1, span), 1) < s.length, 0.0, -1e30)
    for pair in range(pairs):
        key, value = s.key[pair], s.value[pair]
        zero = jnp.zeros_like(key)
        keys = (jnp.where(low, key, zero), jnp.where(low, zero, key))
        value = jnp.concatenate([value, jnp.ones_like(value)], axis=1)
        for rows in blocks_of(s):
            query = s.query[pair, rows, :]
            outs, totals = [], []
            for head in range(2):
                scores = dot(query, keys[head], NT) + bias
                expo = jnp.exp(scores - jnp.max(scores, axis=-1, keepdims=True)).astype(BF16)
                s.expo[2 * pair + head, rows, :] = expo
                product = dot(expo, value)
                outs.append(product[:, :LANES])
                totals.append(product[:, LANES:])
            inv = 1.0 / jnp.where(low, *totals)
            attn = jnp.where(low, *outs) * inv
            s.inv[pair, rows, :] = inv
            s.attn[pair, rows, :] = attn
            s.ctx[rows, pair_lanes(pair)] = attn.astype(BF16)


def attend_backward(s, pair):
    low = lax.broadcasted_iota(jnp.int32, (1, LANES), 1) < LANES // 2
    lanes = pair_lanes(pair)
    key, value, query = s.key[pair], s.value[pair], s.query[pair]
    zero = jnp.zeros_like(key)
    wide = s.ctx[:, lanes].astype(F32) * s.inv[pair]
    terms = wide * s.attn[pair]
    grad = wide.astype(BF16)
    grad_t, query_t = grad.T, query.T
    dquery, dkey, dvalue = 0.0, [], []
    for head in range(2):
        mine = low if head == 0 else ~low
        sub = slice(head * LANES // 2, (head + 1) * LANES // 2)
        delta = jnp.sum(jnp.where(mine, terms, 0.0), axis=-1, keepdims=True)
        expo = s.expo[2 * pair + head]
        dprob = dot(jnp.where(mine, grad, zero), value, NT)
        dscores = (expo.astype(F32) * (dprob - delta)).astype(BF16)
        dquery = dquery + dot(dscores, jnp.where(mine, key, zero))
        dvalue.append(dot(grad_t[sub], expo).astype(BF16))
        dkey.append(dot(query_t[sub], dscores).astype(BF16))
    s.dquery[:, lanes] = (dquery * (LANES // 2) ** -0.5).astype(BF16)
    s.dkey[:, lanes] = jnp.concatenate(dkey, axis=0).T
    s.dvalue[:, lanes] = jnp.concatenate(dvalue, axis=0).T


BLOCK = 256


def blocks_of(s, block=BLOCK):
    return [pl.ds(b * block, block) for b in range(s.tokens.shape[0] // block)]


def project_in(s):
    pairs = s.query.shape[0]
    scale = jnp.asarray((LANES // 2) ** -0.5, BF16)
    for rows in blocks_of(s):
        x = s.tokens[rows, :]
        for weight, target in ((s.w_query, s.query), (s.w_key, s.key), (s.w_value, s.value)):
            y = dot(x, weight[...]).astype(BF16)
            if target is s.query:
                y = y * scale
            for pair in range(pairs):
                target[pair, rows, :] = y[:, pair * LANES : (pair + 1) * LANES]


def first_norm(s):
    for rows in blocks_of(s, 512):
        out = dot(s.ctx[rows, :], s.w_out[...])
        out_low = out.astype(BF16)
        s.out_low[rows, :] = out_low
        act, slope = gelu_parts(dot(out_low, s.down_one[...], NT))
        act = act.astype(BF16)
        s.act_one[rows, :] = act
        s.slope_one[rows, :] = slope
        hidden = s.tokens[rows, :].astype(F32) + out + dot(act, s.up_one[...])
        unit, inverse = norm_forward(hidden)
        s.unit_one[rows, :] = unit
        s.inverse_one[rows, :] = inverse
        normed = unit * s.gain_one[...] + s.bias_one[...]
        s.normed_low[rows, :] = normed.astype(BF16)
        s.total[rows, :] = jnp.zeros_like(normed)


def feed_forward(s):
    for tile in range(s.w_inner.shape[0]):
        for rows in blocks_of(s):
            act, slope = gelu_parts(dot(s.normed_low[rows, :], s.w_inner[tile]))
            s.slope[tile, rows, :] = slope.astype(BF16)
            s.total[rows, :] += dot(act.astype(BF16), s.w_outer[tile])


def vector_slots(width):
    pairs = width // LANES
    per = pl.cdiv(2 * pairs, 2 * GROUP)
    return [
        (2 * side + i // pairs, i % pairs, side, i // per, i % per) for side in range(2) for i in range(2 * pairs)
    ]


def add_vector(s, which, value):
    for vector, piece, side, chunk, row in vector_slots(value.shape[-1]):
        if vector == which:
            s.vectors[side, chunk, row : row + 1, :] += value[:, pair_lanes(piece)]


def second_norm(s):
    for rows in blocks_of(s, 512):
        ffn = s.total[rows, :]
        ffn_low = ffn.astype(BF16)
        act, slope = gelu_parts(dot(ffn_low, s.down_two[...], NT))
        act = act.astype(BF16)
        normed = s.unit_one[rows, :] * s.gain_one[...] + s.bias_one[...]
        hidden = normed + ffn + dot(act, s.up_two[...])
        unit, inverse = norm_forward(hidden)
        s.output[rows, :] = (unit * s.gain_two[...] + s.bias_two[...]).astype(BF16)
        dy = s.cotangent[rows, :].astype(F32)
        add_vector(s, 2, jnp.sum(dy * unit, axis=0, keepdims=True))
        add_vector(s, 3, jnp.sum(dy, axis=0, keepdims=True))
        dh = norm_backward(dy, unit, inverse, s.gain_two[...])
        da = dh.astype(BF16)
        s.grads[3, :, :] += dot(act, da, TN)
        dz = (dot(da, s.up_two[...], NT) * slope).astype(BF16)
        s.grads[2, :, :] += dot(dz, ffn_low, TN)
        s.total[rows, :] = dh
        s.dffn[rows, :] = (dh + dot(dz, s.down_two[...])).astype(BF16)


def feed_backward(s):
    for tile in range(s.w_inner.shape[0]):
        for rows in blocks_of(s):
            du = dot(s.dffn[rows, :], s.w_outer[tile], NT) * s.slope[tile, rows, :].astype(F32)
            s.total[rows, :] += dot(du.astype(BF16), s.w_inner[tile], NT)


def first_norm_backward(s):
    for rows in blocks_of(s):
        dy = s.total[rows, :]
        unit = s.unit_one[rows, :]
        add_vector(s, 0, jnp.sum(dy * unit, axis=0, keepdims=True))
        add_vector(s, 1, jnp.sum(dy, axis=0, keepdims=True))
        dh = norm_backward(dy, unit, s.inverse_one[rows, :], s.gain_one[...])
        s.total[rows, :] = dh
        da = dh.astype(BF16)
        s.grads[1, :, :] += dot(s.act_one[rows, :], da, TN)
        dz = (dot(da, s.up_one[...], NT) * s.slope_one[rows, :]).astype(BF16)
        s.grads[0, :, :] += dot(dz, s.out_low[rows, :], TN)
        dout = (dh + dot(dz, s.down_one[...])).astype(BF16)
        s.ctx[rows, :] = dot(dout, s.w_out[...], NT).astype(BF16)


def project_back(s):
    for rows in blocks_of(s):
        grad = s.total[rows, :] + dot(s.dquery[rows, :], s.w_query[...], NT)
        grad = grad + dot(s.dkey[rows, :], s.w_key[...], NT)
        grad = grad + dot(s.dvalue[rows, :], s.w_value[...], NT)
        s.grad_in[rows, :] = grad.astype(BF16)


PHASES = {
    "project_in": project_in,
    "attend_forward": attend_forward,
    "first_norm": first_norm,
    "feed_forward": feed_forward,
    "second_norm": second_norm,
    "feed_backward": feed_backward,
    "first_norm_backward": first_norm_backward,
    "attend_backward": lambda s: [attend_backward(s, pair) for pair in range(6)],
    "project_back": project_back,
}


def small_shapes(width, adapt):
    flat = ((adapt, width), BF16)
    row = ((1, width), F32)
    return dict(zip(INPUTS[6:], (flat,) * 4 + (row,) * 4))


INPUTS = (
    "w_query", "w_key", "w_value", "w_out", "w_inner", "w_outer",
    "down_one", "up_one", "down_two", "up_two",
    "gain_one", "bias_one", "gain_two", "bias_two",
)
BIG = INPUTS[:6]


def layer_scratch(span, width, hidden, adapt):
    pairs, tiles = width // LANES, hidden // width
    v = pltpu.VMEM
    return {
        "v_w_query": v((width, width), BF16),
        "v_w_key": v((width, width), BF16),
        "v_w_value": v((width, width), BF16),
        "v_w_out": v((width, width), BF16),
        "v_w_inner": v((tiles, width, width), BF16),
        "v_w_outer": v((tiles, width, width), BF16),
        "query": v((pairs, span, LANES), BF16),
        "key": v((pairs, span, LANES), BF16),
        "value": v((pairs, span, LANES), BF16),
        "expo": v((2 * pairs, span, span), BF16),
        "inv": v((pairs, span, LANES), F32),
        "attn": v((pairs, span, LANES), F32),
        "ctx": v((span, width), BF16),
        "out_low": v((span, width), BF16),
        "act_one": v((span, adapt), BF16),
        "slope_one": v((span, adapt), F32),
        "unit_one": v((span, width), F32),
        "inverse_one": v((span, 1), F32),
        "normed_low": v((span, width), BF16),
        "slope": v((tiles, span, width), BF16),
        "total": v((span, width), F32),
        "dffn": v((span, width), BF16),
        "dquery": v((span, width), BF16),
        "dkey": v((span, width), BF16),
        "dvalue": v((span, width), BF16),
    }


class Reduce:
    def __init__(self, s, side, parts, devices, me, refs):
        self.s, self.side = s, side
        self.half, self.pair = lax.rem(me, 2), me // 2
        self.pairs, self.outer = parts // 2, devices // GROUP
        place = lax.axis_index("dp")
        self.inner, self.group = lax.rem(place, GROUP), place // GROUP
        self.send, self.got_near, self.part, self.got_dp, self.got_far, self.full, self.sems = (
            ref.at[side] for ref in refs
        )
        self.near = {"seq": me + 1 - 2 * self.half}
        self.ring = [lax.rem(self.inner + k, GROUP) for k in range(GROUP)]
        self.across = [{"dp": self.group * GROUP + k} for k in self.ring]
        self.far = [
            {
                "seq": lax.rem(self.pair + k % self.pairs, self.pairs) * 2 + self.half,
                "dp": lax.rem(self.group + k // self.pairs, self.outer) * GROUP + self.inner,
            }
            for k in range(self.pairs * self.outer)
        ]

    def greeted(self):
        return [self.near, *self.across[1:], *self.far[1:]]

    def copies(self, stage):
        mine, theirs = self.half * GROUP, (1 - self.half) * GROUP
        if stage == 0:
            moves = [(self.send.at[pl.ds(theirs, GROUP)], self.got_near, self.near)]
        elif stage == 1:
            moves = [(self.part.at[self.ring[k]], self.got_dp.at[k], self.across[k]) for k in range(1, GROUP)]
        elif stage == 2:
            block = self.got_far.at[self.group * self.pairs + self.pair]
            moves = [(block, block, device) for device in self.far[1:]]
        elif stage == 3:
            block = self.full.at[mine + self.inner]
            moves = [(block, block, device) for device in self.across[1:]]
        else:
            block = self.full.at[pl.ds(mine, GROUP)]
            moves = [(block, block, self.near)]
        return [
            pltpu.make_async_remote_copy(
                src_ref=source,
                dst_ref=target,
                send_sem=self.sems.at[0, stage, k],
                recv_sem=self.sems.at[1, stage, k],
                device_id=device,
                device_id_type=MESH,
            )
            for k, (source, target, device) in enumerate(moves)
        ]

    def start(self, stage):
        for copy in self.copies(stage):
            copy.start()

    def finish(self, stage):
        for copy in self.copies(stage):
            copy.wait()

    def first(self):
        grads, vectors = self.s.grads, self.s.vectors
        adapt, width = grads.shape[1:]
        chunks, rows = self.send.shape[:2]
        for c in range(chunks):
            at = c * rows
            matrix = 2 * self.side + at // adapt
            self.send[c, :, :width] = grads[matrix, at % adapt : at % adapt + rows, :].astype(BF16)
            self.send[c, :, width:] = vectors[self.side, c].astype(BF16)
        self.start(0)

    def second(self):
        self.finish(0)
        total = self.send[pl.ds(self.half * GROUP, GROUP)].astype(F32) + self.got_near[...].astype(F32)
        self.part[...] = total.astype(BF16)
        self.start(1)

    def third(self):
        self.finish(1)
        total = self.part[self.inner].astype(F32)
        for k in range(1, GROUP):
            total = total + self.got_dp[k].astype(F32)
        self.got_far[self.group * self.pairs + self.pair] = total.astype(BF16)
        self.start(2)

    def fourth(self):
        self.finish(2)
        total = self.got_far[0].astype(F32)
        for k in range(1, self.pairs * self.outer):
            total = total + self.got_far[k].astype(F32)
        self.full[self.half * GROUP + self.inner] = total.astype(BF16)
        self.start(3)

    def fifth(self):
        self.finish(3)
        self.start(4)


def layer_kernel(parts, devices, per, lengths, tokens, cotangent, *refs):
    s = Refs()
    refs = list(refs)
    for name in INPUTS:
        setattr(s, name, refs.pop(0))
    for name in INPUTS[10:]:
        setattr(s, name, getattr(s, name)[...].reshape(1, -1))
    hbm = {name: getattr(s, name) for name in BIG}
    output, grad_in, full = (refs.pop(0) for _ in range(3))
    for name in layer_scratch(LANES, LANES, LANES, 8):
        setattr(s, name, refs.pop(0))
    s.grads, s.vectors, x_in, dy_in, out_buf, grad_buf = (refs.pop(0) for _ in range(6))
    w_sem, own_sem, send_sem, recv_sem = (refs.pop(0) for _ in range(4))

    me = lax.axis_index("seq")
    rows = tokens.shape[1]
    mine = pl.ds(me * rows, rows)
    near = me + 1 - 2 * lax.rem(me, 2)
    peers = [near] + [
        lax.rem(me // 2 + k, parts // 2) * 2 + core for core in range(2) for k in range(1, parts // 2)
    ]
    refs.insert(5, full)
    one, two = (Reduce(s, side, parts, devices, me, refs) for side in range(2))

    barrier = pltpu.get_barrier_semaphore()
    greeted = [{"seq": peer} for peer in peers] + one.greeted()
    for device in greeted:
        pl.semaphore_signal(barrier, inc=1, device_id=device, device_id_type=MESH)

    width = tokens.shape[2]
    weight_copies = []
    for index, name in enumerate(BIG):
        ref = getattr(s, "v_" + name)
        if name == "w_inner":
            for t in range(ref.shape[0]):
                weight_copies.append(
                    pltpu.make_async_copy(hbm[name].at[:, pl.ds(t * width, width)], ref.at[t], w_sem.at[index, t])
                )
        elif name == "w_outer":
            for t in range(ref.shape[0]):
                weight_copies.append(
                    pltpu.make_async_copy(hbm[name].at[pl.ds(t * width, width), :], ref.at[t], w_sem.at[index, t])
                )
        else:
            weight_copies.append(pltpu.make_async_copy(hbm[name], ref, w_sem.at[index, 0]))
        setattr(s, name, ref)

    pl.semaphore_wait(barrier, len(greeted))

    def move(array, step, peer, slot):
        if array < 2:
            source, target = ((tokens, x_in), (cotangent, dy_in))[array]
            source, target = source.at[step * parts + peer], target.at[step, mine]
        else:
            source, target = ((out_buf, output), (grad_buf, grad_in))[array - 2]
            source, target = source.at[step, pl.ds(peer * rows, rows)], target.at[step * parts + me]
        if slot is None:
            return pltpu.make_async_copy(source, target, own_sem.at[array, step])
        return pltpu.make_async_remote_copy(
            src_ref=source,
            dst_ref=target,
            send_sem=send_sem.at[array, step, peer],
            recv_sem=recv_sem.at[array, step, slot],
            device_id={"seq": peer},
            device_id_type=MESH,
        )

    def start(array, step):
        for peer in peers:
            move(array, step, peer, me).start()
        move(array, step, me, None).start()

    def finish(array, step):
        for peer in peers:
            move(array, step, peer, peer).wait()
        move(array, step, me, None).wait()

    start(0, 0)
    for copy in weight_copies:
        copy.start()
    for ref in (s.grads, s.vectors):
        ref[...] = jnp.zeros_like(ref)
    for copy in weight_copies:
        copy.wait()

    @pl.loop(0, per)
    def _(step):
        more, final = step + 1 < per, step == per - 1
        s.tokens, s.cotangent = x_in.at[step], dy_in.at[step]
        s.output, s.grad_in = out_buf.at[step], grad_buf.at[step]
        s.length = lengths[step * parts + me]
        finish(0, step)

        @pl.when(step == 0)
        def _():
            start(1, 0)

        @pl.when(more)
        def _():
            start(0, step + 1)

        project_in(s)
        attend_forward(s)
        first_norm(s)
        feed_forward(s)
        finish(1, step)

        @pl.when(more)
        def _():
            start(1, step + 1)

        at_end = pl.when(final)
        second_norm(s)
        start(2, step)

        @at_end
        def _():
            two.first()
            two.second()

        feed_backward(s)
        first_norm_backward(s)

        @at_end
        def _():
            one.first()
            two.third()
            one.second()

        for pair in range(s.query.shape[0]):
            attend_backward(s, pair)

        @at_end
        def _():
            one.third()
            two.fourth()

        project_back(s)
        start(3, step)

    one.fourth()
    two.fifth()
    one.fifth()
    one.finish(4)
    two.finish(4)

    @pl.loop(0, per)
    def _(step):
        finish(2, step)
        finish(3, step)


def tail_kernel(output, grad_in, full, output_out, grad_in_out, *grads):
    output_out[...] = output[...]
    grad_in_out[...] = grad_in[...].astype(F32)

    @pl.when(pl.program_id(0) == 0)
    def _():
        matrices, vectors = grads[:4], grads[4:]
        adapt, width = matrices[0].shape
        chunks, rows = full.shape[1:3]
        for side in range(2):
            for c in range(chunks):
                at = c * rows
                matrix = matrices[2 * side + at // adapt]
                matrix[at % adapt : at % adapt + rows, :] = full[side, c, :, :width].astype(F32)
        tails = full[:, :, :, width:].astype(F32)
        for vector, piece, side, chunk, row in vector_slots(width):
            vectors[vector][pair_lanes(piece)] = tails[side, chunk, row]


def per_device(parts, devices, tokens, lengths, cotangent, *params):
    batch, rows, width = tokens.shape
    hidden, adapt = params[4].shape[1], params[6].shape[1]
    per, span = batch // parts, parts * rows
    chunks, chunk_rows = 2 * GROUP, adapt // GROUP
    far = parts // 2 * (devices // GROUP)
    params = list(params)
    params[6], params[8] = params[6].T, params[8].T
    vmem = pl.BlockSpec(memory_space=pltpu.VMEM)
    anywhere = pl.BlockSpec(memory_space=pl.ANY)
    dma = pltpu.SemaphoreType.DMA
    chunk = (chunk_rows, width + LANES)
    scratch = [
        *layer_scratch(span, width, hidden, adapt).values(),
        pltpu.VMEM((4, adapt, width), F32),
        pltpu.VMEM((2, chunks, chunk_rows, LANES), F32),
        *[pltpu.VMEM((per, span, width), BF16)] * 4,
        dma((len(BIG), hidden // width)),
        dma((4, per)),
        dma((4, per, parts)),
        dma((4, per, parts)),
        pltpu.VMEM((2, chunks, *chunk), BF16),
        *[pltpu.VMEM((2, GROUP, *chunk), BF16)] * 3,
        pltpu.VMEM((2, far, *chunk), BF16),
        dma((2, 2, 5, max(GROUP, far))),
    ]
    moved = jax.ShapeDtypeStruct((batch, rows, width), BF16)
    summed = jax.ShapeDtypeStruct((2, chunks, *chunk), BF16)
    output, grad_in, full = pl.pallas_call(
        functools.partial(layer_kernel, parts, devices, per),
        out_shape=(moved, moved, summed),
        in_specs=[pl.BlockSpec(memory_space=pltpu.SMEM)]
        + [anywhere] * 2
        + [anywhere if name in BIG else vmem for name in INPUTS],
        out_specs=(anywhere, anywhere, vmem),
        scratch_shapes=scratch,
        compiler_params=pltpu.CompilerParams(
            collective_id=0, has_side_effects=True, vmem_limit_bytes=62 * 2**20
        ),
        name="layer",
    )(lengths, tokens, cotangent, *params)
    block = pl.BlockSpec((batch // 2, rows, width), lambda i: (i, 0, 0))
    whole = [pl.BlockSpec((adapt, width), lambda i: (0, 0))] * 4 + [pl.BlockSpec((width,), lambda i: (0,))] * 4
    output, grad_in, down_one, up_one, down_two, up_two, *vectors = pl.pallas_call(
        tail_kernel,
        grid=(2,),
        out_shape=(
            moved,
            jax.ShapeDtypeStruct((batch, rows, width), F32),
            *[jax.ShapeDtypeStruct((adapt, width), F32)] * 4,
            *[jax.ShapeDtypeStruct((width,), F32)] * 4,
        ),
        in_specs=[block, block, pl.BlockSpec(summed.shape, lambda i: (0, 0, 0, 0))],
        out_specs=(block, block, *whole),
        name="tail",
    )(output, grad_in, full)
    return (output, grad_in, down_one.T, up_one, down_two.T, up_two, *vectors)


def solution(mesh):
    split = P("dp", "seq", None)
    return jax.shard_map(
        functools.partial(per_device, mesh.shape["seq"], mesh.shape["dp"]),
        mesh=mesh,
        in_specs=(split, P("dp"), split) + (P(),) * 14,
        out_specs=(split, split) + (P(),) * 8,
        check_vma=False,
    )
```

```python
import functools

import jax
import jax.numpy as jnp
from jax import lax
from jax.experimental import pallas as pl
from jax.experimental.pallas import tpu as pltpu
from jax.sharding import PartitionSpec as P

HEADS = 12
EPS = 1e-06
F32 = jnp.float32
BF16 = jnp.bfloat16
NN = (((1,), (0,)), ((), ()))
NT = (((1,), (1,)), ((), ()))
TN = (((0,), (0,)), ((), ()))
MESH = pl.DeviceIdType.MESH
LANES = 128
GROUP = 8


def dot(left, right, dims=NN):
    return lax.dot_general(left, right, dims, preferred_element_type=F32)


def gelu_parts(value):
    phi = 0.5 + 0.5 * lax.erf(value * 0.7071067811865476)
    scaled = value * jnp.exp(value * value * -0.5) * 0.3989422804014327
    return value * phi, phi + scaled


def row_mean(value):
    return jnp.sum(value, axis=-1, keepdims=True) * (1.0 / value.shape[-1])


def norm_forward(hidden):
    centred = hidden - row_mean(hidden)
    inverse = lax.rsqrt(row_mean(centred * centred) + EPS)
    return centred * inverse, inverse


def norm_backward(grad, unit, inverse, gain):
    scaled = grad * gain
    inner = scaled - row_mean(scaled) - unit * row_mean(scaled * unit)
    return inner * inverse


class Refs:
    pass


def pair_lanes(pair):
    return slice(pair * LANES, (pair + 1) * LANES)


def attend_forward(s):
    pairs, span = s.query.shape[:2]
    low = lax.broadcasted_iota(jnp.int32, (1, LANES), 1) < LANES // 2
    column = lax.broadcasted_iota(jnp.int32, (1, span), 1)
    position = column
    for at, shift in s.shifts:
        position = jnp.where(column >= at, column + shift, position)
    bias = jnp.where(position < s.length, 0.0, -1e30)
    for pair in range(pairs):
        key, value = s.key[pair], s.value[pair]
        zero = jnp.zeros_like(key)
        keys = (jnp.where(low, key, zero), jnp.where(low, zero, key))
        value = jnp.concatenate([value, jnp.ones_like(value)], axis=1)
        for rows in blocks_of(s):
            query = s.query[pair, rows, :]
            outs, totals = [], []
            for head in range(2):
                scores = dot(query, keys[head], NT) + bias
                expo = jnp.exp(scores - jnp.max(scores, axis=-1, keepdims=True)).astype(BF16)
                s.expo[2 * pair + head, rows, :] = expo
                product = dot(expo, value)
                outs.append(product[:, :LANES])
                totals.append(product[:, LANES:])
            inv = 1.0 / jnp.where(low, *totals)
            attn = jnp.where(low, *outs) * inv
            s.inv[pair, rows, :] = inv
            s.attn[pair, rows, :] = attn
            s.ctx[rows, pair_lanes(pair)] = attn.astype(BF16)


def attend_backward(s, pair):
    low = lax.broadcasted_iota(jnp.int32, (1, LANES), 1) < LANES // 2
    lanes = pair_lanes(pair)
    key, value, query = s.key[pair], s.value[pair], s.query[pair]
    zero = jnp.zeros_like(key)
    wide = s.ctx[:, lanes].astype(F32) * s.inv[pair]
    terms = wide * s.attn[pair]
    grad = wide.astype(BF16)
    grad_t, query_t = grad.T, query.T
    dquery, dkey, dvalue = 0.0, [], []
    for head in range(2):
        mine = low if head == 0 else ~low
        sub = slice(head * LANES // 2, (head + 1) * LANES // 2)
        delta = jnp.sum(jnp.where(mine, terms, 0.0), axis=-1, keepdims=True)
        expo = s.expo[2 * pair + head]
        dprob = dot(jnp.where(mine, grad, zero), value, NT)
        dscores = (expo.astype(F32) * (dprob - delta)).astype(BF16)
        dquery = dquery + dot(dscores, jnp.where(mine, key, zero))
        dvalue.append(dot(grad_t[sub], expo).astype(BF16))
        dkey.append(dot(query_t[sub], dscores).astype(BF16))
    grads = (
        (dquery * (LANES // 2) ** -0.5).astype(BF16),
        jnp.concatenate(dkey, axis=0).T,
        jnp.concatenate(dvalue, axis=0).T,
    )
    for which, grad in enumerate(grads):
        s.near_grads[which, :, lanes] = grad[: s.near_rows]
        s.far_grads[which, :, lanes] = grad[s.near_rows :]


BLOCK = 256


def blocks_of(s, block=BLOCK):
    return [pl.ds(b * block, block) for b in range(s.tokens.shape[0] // block)]


def far_blocks(s):
    near, span = s.near_rows, s.tokens.shape[0]
    return [pl.ds(at, BLOCK) for at in range(near, span, BLOCK)]


def project_in(s, blocks):
    pairs = s.query.shape[0]
    scale = jnp.asarray((LANES // 2) ** -0.5, BF16)
    for rows in blocks:
        x = s.tokens[rows, :]
        for weight, target in ((s.w_query, s.query), (s.w_key, s.key), (s.w_value, s.value)):
            y = dot(x, weight[...]).astype(BF16)
            if target is s.query:
                y = y * scale
            for pair in range(pairs):
                target[pair, rows, :] = y[:, pair * LANES : (pair + 1) * LANES]


def first_norm(s):
    for rows in blocks_of(s, 512):
        out = dot(s.ctx[rows, :], s.w_out[...])
        out_low = out.astype(BF16)
        s.out_low[rows, :] = out_low
        act, slope = gelu_parts(dot(out_low, s.down_one[...], NT))
        act = act.astype(BF16)
        s.act_one[rows, :] = act
        s.slope_one[rows, :] = slope
        hidden = s.tokens[rows, :].astype(F32) + out + dot(act, s.up_one[...])
        unit, inverse = norm_forward(hidden)
        s.unit_one[rows, :] = unit
        s.inverse_one[rows, :] = inverse
        normed = unit * s.gain_one[...] + s.bias_one[...]
        s.normed_low[rows, :] = normed.astype(BF16)
        s.total[rows, :] = jnp.zeros_like(normed)


def feed_forward(s):
    for tile in range(s.w_inner.shape[0]):
        for rows in blocks_of(s):
            act, slope = gelu_parts(dot(s.normed_low[rows, :], s.w_inner[tile]))
            s.slope[tile, rows, :] = slope.astype(BF16)
            s.total[rows, :] += dot(act.astype(BF16), s.w_outer[tile])


def vector_slots(width):
    pairs = width // LANES
    per = pl.cdiv(2 * pairs, 2 * GROUP)
    return [
        (2 * side + i // pairs, i % pairs, side, i // per, i % per) for side in range(2) for i in range(2 * pairs)
    ]


def add_vector(s, which, value):
    for vector, piece, side, chunk, row in vector_slots(value.shape[-1]):
        if vector == which:
            s.vectors[side, chunk, row : row + 1, :] += value[:, pair_lanes(piece)]


def second_norm(s):
    for rows in blocks_of(s, 512):
        ffn = s.total[rows, :]
        ffn_low = ffn.astype(BF16)
        act, slope = gelu_parts(dot(ffn_low, s.down_two[...], NT))
        act = act.astype(BF16)
        normed = s.unit_one[rows, :] * s.gain_one[...] + s.bias_one[...]
        hidden = normed + ffn + dot(act, s.up_two[...])
        unit, inverse = norm_forward(hidden)
        dy = s.cotangent[rows, :].astype(F32)
        s.output[rows, :] = (unit * s.gain_two[...] + s.bias_two[...]).astype(BF16)
        add_vector(s, 2, jnp.sum(dy * unit, axis=0, keepdims=True))
        add_vector(s, 3, jnp.sum(dy, axis=0, keepdims=True))
        dh = norm_backward(dy, unit, inverse, s.gain_two[...])
        da = dh.astype(BF16)
        s.grads[3, :, :] += dot(act, da, TN)
        dz = (dot(da, s.up_two[...], NT) * slope).astype(BF16)
        s.grads[2, :, :] += dot(dz, ffn_low, TN)
        s.total[rows, :] = dh
        s.dffn[rows, :] = (dh + dot(dz, s.down_two[...])).astype(BF16)


def feed_backward(s):
    for tile in range(s.w_inner.shape[0]):
        for rows in blocks_of(s):
            du = dot(s.dffn[rows, :], s.w_outer[tile], NT) * s.slope[tile, rows, :].astype(F32)
            s.total[rows, :] += dot(du.astype(BF16), s.w_inner[tile], NT)


def first_norm_backward(s):
    for rows in [pl.ds(0, s.near_rows), *far_blocks(s)]:
        dy = s.total[rows, :]
        unit = s.unit_one[rows, :]
        add_vector(s, 0, jnp.sum(dy * unit, axis=0, keepdims=True))
        add_vector(s, 1, jnp.sum(dy, axis=0, keepdims=True))
        dh = norm_backward(dy, unit, s.inverse_one[rows, :], s.gain_one[...])
        if rows.start == 0:
            s.near_total[...] = dh
        else:
            s.total[rows, :] = dh
        da = dh.astype(BF16)
        s.grads[1, :, :] += dot(s.act_one[rows, :], da, TN)
        dz = (dot(da, s.up_one[...], NT) * s.slope_one[rows, :]).astype(BF16)
        s.grads[0, :, :] += dot(dz, s.out_low[rows, :], TN)
        dout = (dh + dot(dz, s.down_one[...])).astype(BF16)
        s.ctx[rows, :] = dot(dout, s.w_out[...], NT).astype(BF16)


def project_back(s, total, grads, target):
    weights = (s.w_query, s.w_key, s.w_value)
    rows = target.shape[0]
    for block in [pl.ds(at, min(BLOCK, rows)) for at in range(0, rows, BLOCK)]:
        grad = total[block, :]
        for which, weight in enumerate(weights):
            grad = grad + dot(grads[which, block, :], weight[...], NT)
        target[block, :] = grad.astype(BF16)


INPUTS = (
    "w_query", "w_key", "w_value", "w_out", "w_inner", "w_outer",
    "down_one", "up_one", "down_two", "up_two",
    "gain_one", "bias_one", "gain_two", "bias_two",
)
BIG = INPUTS[:6]


def layer_scratch(span, near, per, width, hidden, adapt):
    pairs, tiles = width // LANES, hidden // width
    v = pltpu.VMEM
    return {
        "v_w_query": v((width, width), BF16),
        "v_w_key": v((width, width), BF16),
        "v_w_value": v((width, width), BF16),
        "v_w_out": v((width, width), BF16),
        "v_w_inner": v((tiles, width, width), BF16),
        "v_w_outer": v((tiles, width, width), BF16),
        "all_query": v((per, pairs, span, LANES), BF16),
        "all_key": v((per, pairs, span, LANES), BF16),
        "all_value": v((per, pairs, span, LANES), BF16),
        "expo": v((2 * pairs, span, span), BF16),
        "inv": v((pairs, span, LANES), F32),
        "attn": v((pairs, span, LANES), F32),
        "ctx": v((span, width), BF16),
        "out_low": v((span, width), BF16),
        "act_one": v((span, adapt), BF16),
        "slope_one": v((span, adapt), F32),
        "unit_one": v((span, width), F32),
        "inverse_one": v((span, 1), F32),
        "normed_low": v((span, width), BF16),
        "slope": v((tiles, span, width), BF16),
        "total": v((span, width), F32),
        "dffn": v((span, width), BF16),
        "all_near_grads": v((per, 3, near, width), BF16),
        "all_near_total": v((per, near, width), F32),
        "far_grads": v((3, span - near, width), BF16),
    }


class Reduce:
    def __init__(self, s, side, parts, devices, me, refs):
        self.s, self.side = s, side
        self.half, self.pair = lax.rem(me, 2), me // 2
        self.pairs, self.outer = parts // 2, devices // GROUP
        place = lax.axis_index("dp")
        self.inner, self.group = lax.rem(place, GROUP), place // GROUP
        self.send, self.got_near, self.part, self.got_dp, self.got_far, self.full, self.sems = (
            ref.at[side] for ref in refs
        )
        self.near = {"seq": me + 1 - 2 * self.half}
        self.ring = [lax.rem(self.inner + k, GROUP) for k in range(GROUP)]
        self.across = [{"dp": self.group * GROUP + k} for k in self.ring]
        self.far = [
            {
                "seq": lax.rem(self.pair + k % self.pairs, self.pairs) * 2 + self.half,
                "dp": lax.rem(self.group + k // self.pairs, self.outer) * GROUP + self.inner,
            }
            for k in range(self.pairs * self.outer)
        ]

    def greeted(self):
        return [self.near, *self.across[1:], *self.far[1:]]

    def copies(self, stage):
        mine, theirs = self.half * GROUP, (1 - self.half) * GROUP
        if stage == 0:
            moves = [(self.send.at[pl.ds(theirs, GROUP)], self.got_near, self.near)]
        elif stage == 1:
            moves = [(self.part.at[self.ring[k]], self.got_dp.at[k], self.across[k]) for k in range(1, GROUP)]
        elif stage == 2:
            block = self.got_far.at[self.group * self.pairs + self.pair]
            moves = [(block, block, device) for device in self.far[1:]]
        elif stage == 3:
            block = self.full.at[mine + self.inner]
            moves = [(block, block, device) for device in self.across[1:]]
        else:
            block = self.full.at[pl.ds(mine, GROUP)]
            moves = [(block, block, self.near)]
        return [
            pltpu.make_async_remote_copy(
                src_ref=source,
                dst_ref=target,
                send_sem=self.sems.at[0, stage, k],
                recv_sem=self.sems.at[1, stage, k],
                device_id=device,
                device_id_type=MESH,
            )
            for k, (source, target, device) in enumerate(moves)
        ]

    def start(self, stage):
        for copy in self.copies(stage):
            copy.start()

    def finish(self, stage):
        for copy in self.copies(stage):
            copy.wait()

    def first(self):
        grads, vectors = self.s.grads, self.s.vectors
        adapt, width = grads.shape[1:]
        chunks, rows = self.send.shape[:2]
        for c in range(chunks):
            at = c * rows
            matrix = 2 * self.side + at // adapt
            self.send[c, :, :width] = grads[matrix, at % adapt : at % adapt + rows, :].astype(BF16)
            self.send[c, :, width:] = vectors[self.side, c].astype(BF16)
        self.start(0)

    def second(self):
        self.finish(0)
        total = self.send[pl.ds(self.half * GROUP, GROUP)].astype(F32) + self.got_near[...].astype(F32)
        self.part[...] = total.astype(BF16)
        self.start(1)

    def third(self):
        self.finish(1)
        total = self.part[self.inner].astype(F32)
        for k in range(1, GROUP):
            total = total + self.got_dp[k].astype(F32)
        self.got_far[self.group * self.pairs + self.pair] = total.astype(BF16)
        self.start(2)

    def fourth(self):
        self.finish(2)
        total = self.got_far[0].astype(F32)
        for k in range(1, self.pairs * self.outer):
            total = total + self.got_far[k].astype(F32)
        self.full[self.half * GROUP + self.inner] = total.astype(BF16)
        self.start(3)

    def fifth(self):
        self.finish(3)
        self.start(4)


def layer_kernel(parts, devices, per, lengths, tokens, cotangent, *refs):
    s = Refs()
    refs = list(refs)
    for name in INPUTS:
        setattr(s, name, refs.pop(0))
    for name in INPUTS[10:]:
        setattr(s, name, getattr(s, name)[...].reshape(1, -1))
    hbm = {name: getattr(s, name) for name in BIG}
    output, grad_in, full = (refs.pop(0) for _ in range(3))
    for name in layer_scratch(LANES, 8, 1, LANES, LANES, 8):
        setattr(s, name, refs.pop(0))
    s.grads, s.vectors, x_in, dy_in = (refs.pop(0) for _ in range(4))
    w_sem, own_sem, send_sem, recv_sem = (refs.pop(0) for _ in range(4))

    me = lax.axis_index("seq")
    rows = tokens.shape[1]
    couples = parts // 2
    core, couple = lax.rem(me, 2), me // 2
    s.near_rows = 2 * rows
    s.shifts = []
    for k in range(couples):
        s.shifts.append((k * 2 * rows, (lax.rem(couple + k, couples) - k) * 2 * rows))
    near = [(0, 1 - core)]
    far = [(k, c) for c in range(2) for k in range(1, couples)]

    def index_of(peer):
        k, c = peer
        return lax.rem(couple + k, couples) * 2 + c

    refs.insert(5, full)
    one, two = (Reduce(s, side, parts, devices, me, refs) for side in range(2))

    barrier = pltpu.get_barrier_semaphore()
    greeted = [{"seq": index_of(peer)} for peer in near + far] + one.greeted()
    for device in greeted:
        pl.semaphore_signal(barrier, inc=1, device_id=device, device_id_type=MESH)

    width = tokens.shape[2]
    weight_copies = []
    for index, name in enumerate(BIG):
        ref = getattr(s, "v_" + name)
        if name == "w_inner":
            for t in range(ref.shape[0]):
                weight_copies.append(
                    pltpu.make_async_copy(hbm[name].at[:, pl.ds(t * width, width)], ref.at[t], w_sem.at[index, t])
                )
        elif name == "w_outer":
            for t in range(ref.shape[0]):
                weight_copies.append(
                    pltpu.make_async_copy(hbm[name].at[pl.ds(t * width, width), :], ref.at[t], w_sem.at[index, t])
                )
        else:
            weight_copies.append(pltpu.make_async_copy(hbm[name], ref, w_sem.at[index, 0]))
        setattr(s, name, ref)

    pl.semaphore_wait(barrier, len(greeted))

    def move(array, step, peer, slot):
        k, c = (0, core) if peer is None else peer
        other = me if peer is None else index_of(peer)
        outside, inside = ((tokens, x_in), (cotangent, dy_in), (output, dy_in), (grad_in, x_in))[array]
        if array < 2:
            source = outside.at[step * parts + other]
            target = inside.at[step, pl.ds((couples - k) % couples * 2 * rows + core * rows, rows)]
        else:
            source = inside.at[step, pl.ds(k * 2 * rows + c * rows, rows)]
            target = outside.at[step * parts + me]
        if peer is None:
            return pltpu.make_async_copy(source, target, own_sem.at[array, step])
        return pltpu.make_async_remote_copy(
            src_ref=source,
            dst_ref=target,
            send_sem=send_sem.at[array, step, other],
            recv_sem=recv_sem.at[array, step, other if slot is None else slot],
            device_id={"seq": other},
            device_id_type=MESH,
        )

    def start(array, step, peers):
        for peer in peers:
            move(array, step, peer, me).start()

    def finish(array, step, peers):
        for peer in peers:
            move(array, step, peer, None).wait()

    near = near + [None]
    everyone = far + near

    def view(step):
        s.tokens, s.cotangent = x_in.at[step], dy_in.at[step]
        s.query, s.key, s.value = (ref.at[step] for ref in (s.all_query, s.all_key, s.all_value))
        s.near_grads, s.near_total = s.all_near_grads.at[step], s.all_near_total.at[step]
        s.output = s.cotangent
        s.length = lengths[step * parts + me]

    near_rows, far_rows = pl.ds(0, s.near_rows), pl.ds(s.near_rows, x_in.shape[1] - s.near_rows)
    start(0, 0, far)
    for step in range(per):
        start(0, step, near)
    for copy in weight_copies:
        copy.start()
    for ref in (s.grads, s.vectors):
        ref[...] = jnp.zeros_like(ref)
    for copy in weight_copies[:3]:
        copy.wait()

    @pl.loop(0, per)
    def _(step):
        view(step)
        finish(0, step, near)
        project_in(s, [near_rows])

    for copy in weight_copies[3:]:
        copy.wait()

    @pl.loop(0, per)
    def _(step):
        more, final = step + 1 < per, step == per - 1
        view(step)
        finish(0, step, far)

        @pl.when(step == 0)
        def _():
            start(1, 0, everyone)

        @pl.when(more)
        def _():
            start(0, step + 1, far)

        project_in(s, far_blocks(s))
        attend_forward(s)
        first_norm(s)
        feed_forward(s)
        finish(1, step, everyone)

        @pl.when(more)
        def _():
            start(1, step + 1, everyone)

        at_end = pl.when(final)
        second_norm(s)
        start(2, step, everyone)

        @at_end
        def _():
            two.first()
            two.second()

        feed_backward(s)
        first_norm_backward(s)

        @at_end
        def _():
            one.first()
            two.third()
            one.second()

        for pair in range(s.query.shape[0]):
            attend_backward(s, pair)

        @at_end
        def _():
            one.third()
            two.fourth()

        project_back(s, s.total.at[far_rows], s.far_grads, x_in.at[step, far_rows])
        start(3, step, far)

    for step in range(per):
        view(step)
        project_back(s, s.near_total, s.near_grads, x_in.at[step, near_rows])
        start(3, step, near)
        if step == min(1, per - 1):
            one.fourth()
            two.fifth()
    one.fifth()
    one.finish(4)
    two.finish(4)

    @pl.loop(0, per)
    def _(step):
        finish(2, step, everyone)
        finish(3, step, everyone)


def tail_kernel(output, grad_in, full, output_out, grad_in_out, *grads):
    output_out[...] = output[...]
    grad_in_out[...] = grad_in[...].astype(F32)

    @pl.when(pl.program_id(0) == 0)
    def _():
        matrices, vectors = grads[:4], grads[4:]
        adapt, width = matrices[0].shape
        chunks, rows = full.shape[1:3]
        for side in range(2):
            for c in range(chunks):
                at = c * rows
                matrix = matrices[2 * side + at // adapt]
                matrix[at % adapt : at % adapt + rows, :] = full[side, c, :, :width].astype(F32)
        tails = full[:, :, :, width:].astype(F32)
        for vector, piece, side, chunk, row in vector_slots(width):
            vectors[vector][pair_lanes(piece)] = tails[side, chunk, row]


def per_device(parts, devices, tokens, lengths, cotangent, *params):
    batch, rows, width = tokens.shape
    hidden, adapt = params[4].shape[1], params[6].shape[1]
    per, span = batch // parts, parts * rows
    chunks, chunk_rows = 2 * GROUP, adapt // GROUP
    far = parts // 2 * (devices // GROUP)
    params = list(params)
    params[6], params[8] = params[6].T, params[8].T
    vmem = pl.BlockSpec(memory_space=pltpu.VMEM)
    anywhere = pl.BlockSpec(memory_space=pl.ANY)
    dma = pltpu.SemaphoreType.DMA
    chunk = (chunk_rows, width + LANES)
    scratch = [
        *layer_scratch(span, 2 * rows, per, width, hidden, adapt).values(),
        pltpu.VMEM((4, adapt, width), F32),
        pltpu.VMEM((2, chunks, chunk_rows, LANES), F32),
        *[pltpu.VMEM((per, span, width), BF16)] * 2,
        dma((len(BIG), hidden // width)),
        dma((4, per)),
        dma((4, per, parts)),
        dma((4, per, parts)),
        pltpu.VMEM((2, chunks, *chunk), BF16),
        *[pltpu.VMEM((2, GROUP, *chunk), BF16)] * 3,
        pltpu.VMEM((2, far, *chunk), BF16),
        dma((2, 2, 5, max(GROUP, far))),
    ]
    moved = jax.ShapeDtypeStruct((batch, rows, width), BF16)
    summed = jax.ShapeDtypeStruct((2, chunks, *chunk), BF16)
    output, grad_in, full = pl.pallas_call(
        functools.partial(layer_kernel, parts, devices, per),
        out_shape=(moved, moved, summed),
        in_specs=[pl.BlockSpec(memory_space=pltpu.SMEM)]
        + [anywhere] * 2
        + [anywhere if name in BIG else vmem for name in INPUTS],
        out_specs=(anywhere, anywhere, vmem),
        scratch_shapes=scratch,
        compiler_params=pltpu.CompilerParams(
            collective_id=0, has_side_effects=True, vmem_limit_bytes=62 * 2**20
        ),
        name="layer",
    )(lengths, tokens, cotangent, *params)
    block = pl.BlockSpec((batch // 2, rows, width), lambda i: (i, 0, 0))
    whole = [pl.BlockSpec((adapt, width), lambda i: (0, 0))] * 4 + [pl.BlockSpec((width,), lambda i: (0,))] * 4
    output, grad_in, down_one, up_one, down_two, up_two, *vectors = pl.pallas_call(
        tail_kernel,
        grid=(2,),
        out_shape=(
            moved,
            jax.ShapeDtypeStruct((batch, rows, width), F32),
            *[jax.ShapeDtypeStruct((adapt, width), F32)] * 4,
            *[jax.ShapeDtypeStruct((width,), F32)] * 4,
        ),
        in_specs=[block, block, pl.BlockSpec(summed.shape, lambda i: (0, 0, 0, 0))],
        out_specs=(block, block, *whole),
        name="tail",
    )(output, grad_in, full)
    return (output, grad_in, down_one.T, up_one, down_two.T, up_two, *vectors)


def solution(mesh):
    split = P("dp", "seq", None)
    return jax.shard_map(
        functools.partial(per_device, mesh.shape["seq"], mesh.shape["dp"]),
        mesh=mesh,
        in_specs=(split, P("dp"), split) + (P(),) * 14,
        out_specs=(split, split) + (P(),) * 8,
        check_vma=False,
    )
```

```python
import functools

import jax
import jax.numpy as jnp
from jax import lax
from jax.experimental import pallas as pl
from jax.experimental.pallas import tpu as pltpu
from jax.sharding import PartitionSpec as P

HEADS = 12
EPS = 1e-06
F32 = jnp.float32
BF16 = jnp.bfloat16
NN = (((1,), (0,)), ((), ()))
NT = (((1,), (1,)), ((), ()))
TN = (((0,), (0,)), ((), ()))
MESH = pl.DeviceIdType.MESH
LANES = 128
GROUP = 8


def dot(left, right, dims=NN):
    return lax.dot_general(left, right, dims, preferred_element_type=F32)


def gelu_parts(value):
    phi = 0.5 + 0.5 * lax.erf(value * 0.7071067811865476)
    scaled = value * jnp.exp(value * value * -0.5) * 0.3989422804014327
    return value * phi, phi + scaled


def row_mean(value):
    return jnp.sum(value, axis=-1, keepdims=True) * (1.0 / value.shape[-1])


def norm_forward(hidden):
    centred = hidden - row_mean(hidden)
    inverse = lax.rsqrt(row_mean(centred * centred) + EPS)
    return centred * inverse, inverse


def norm_backward(grad, unit, inverse, gain):
    scaled = grad * gain
    inner = scaled - row_mean(scaled) - unit * row_mean(scaled * unit)
    return inner * inverse


class Refs:
    pass


def pair_lanes(pair):
    return slice(pair * LANES, (pair + 1) * LANES)


def attend_forward(s):
    pairs, span = s.query.shape[:2]
    low = lax.broadcasted_iota(jnp.int32, (1, LANES), 1) < LANES // 2
    column = lax.broadcasted_iota(jnp.int32, (1, span), 1)
    position = column
    for at, shift in s.shifts:
        position = jnp.where(column >= at, column + shift, position)
    bias = jnp.where(position < s.length, 0.0, -1e30)
    for pair in range(pairs):
        key, value = s.key[pair], s.value[pair]
        zero = jnp.zeros_like(key)
        keys = (jnp.where(low, key, zero), jnp.where(low, zero, key))
        value = jnp.concatenate([value, jnp.ones_like(value)], axis=1)
        for rows in blocks_of(s):
            query = s.query[pair, rows, :]
            outs, totals = [], []
            for head in range(2):
                scores = dot(query, keys[head], NT) + bias
                expo = jnp.exp(scores - jnp.max(scores, axis=-1, keepdims=True)).astype(BF16)
                s.expo[2 * pair + head, rows, :] = expo
                product = dot(expo, value)
                outs.append(product[:, :LANES])
                totals.append(product[:, LANES:])
            inv = 1.0 / jnp.where(low, *totals)
            attn = jnp.where(low, *outs) * inv
            s.inv[pair, rows, :] = inv
            s.attn[pair, rows, :] = attn
            s.ctx[rows, pair_lanes(pair)] = attn.astype(BF16)


def attend_backward(s, pair):
    low = lax.broadcasted_iota(jnp.int32, (1, LANES), 1) < LANES // 2
    lanes = pair_lanes(pair)
    key, value, query = s.key[pair], s.value[pair], s.query[pair]
    zero = jnp.zeros_like(key)
    wide = s.ctx[:, lanes].astype(F32) * s.inv[pair]
    terms = wide * s.attn[pair]
    grad = wide.astype(BF16)
    grad_t, query_t = grad.T, query.T
    dquery, dkey, dvalue = 0.0, [], []
    for head in range(2):
        mine = low if head == 0 else ~low
        sub = slice(head * LANES // 2, (head + 1) * LANES // 2)
        delta = jnp.sum(jnp.where(mine, terms, 0.0), axis=-1, keepdims=True)
        expo = s.expo[2 * pair + head]
        dprob = dot(jnp.where(mine, grad, zero), value, NT)
        dscores = (expo.astype(F32) * (dprob - delta)).astype(BF16)
        dquery = dquery + dot(dscores, jnp.where(mine, key, zero))
        dvalue.append(dot(grad_t[sub], expo).astype(BF16))
        dkey.append(dot(query_t[sub], dscores).astype(BF16))
    grads = (
        (dquery * (LANES // 2) ** -0.5).astype(BF16),
        jnp.concatenate(dkey, axis=0).T,
        jnp.concatenate(dvalue, axis=0).T,
    )
    for which, grad in enumerate(grads):
        s.near_grads[which, :, lanes] = grad[: s.near_rows]
        s.far_grads[which, :, lanes] = grad[s.near_rows :]


BLOCK = 256


def blocks_of(s, block=BLOCK):
    return [pl.ds(b * block, block) for b in range(s.tokens.shape[0] // block)]


def far_blocks(s):
    near, span = s.near_rows, s.tokens.shape[0]
    return [pl.ds(at, BLOCK) for at in range(near, span, BLOCK)]


def project_in(s, blocks):
    pairs = s.query.shape[0]
    scale = jnp.asarray((LANES // 2) ** -0.5, BF16)
    for rows in blocks:
        x = s.tokens[rows, :]
        for weight, target in ((s.w_query, s.query), (s.w_key, s.key), (s.w_value, s.value)):
            y = dot(x, weight[...]).astype(BF16)
            if target is s.query:
                y = y * scale
            for pair in range(pairs):
                target[pair, rows, :] = y[:, pair * LANES : (pair + 1) * LANES]


def first_norm(s):
    for rows in blocks_of(s, 512):
        out = dot(s.ctx[rows, :], s.w_out[...])
        out_low = out.astype(BF16)
        s.out_low[rows, :] = out_low
        act, slope = gelu_parts(dot(out_low, s.down_one[...], NT))
        act = act.astype(BF16)
        s.act_one[rows, :] = act
        s.slope_one[rows, :] = slope
        hidden = s.tokens[rows, :].astype(F32) + out + dot(act, s.up_one[...])
        unit, inverse = norm_forward(hidden)
        s.unit_one[rows, :] = unit
        s.inverse_one[rows, :] = inverse
        normed = unit * s.gain_one[...] + s.bias_one[...]
        s.normed_low[rows, :] = normed.astype(BF16)
        s.total[rows, :] = jnp.zeros_like(normed)


def feed_forward(s):
    for tile in range(s.w_inner.shape[0]):
        for rows in blocks_of(s):
            act, slope = gelu_parts(dot(s.normed_low[rows, :], s.w_inner[tile]))
            s.slope[tile, rows, :] = slope.astype(BF16)
            s.total[rows, :] += dot(act.astype(BF16), s.w_outer[tile])


def vector_slots(width):
    pairs = width // LANES
    per = pl.cdiv(2 * pairs, 2 * GROUP)
    return [
        (2 * side + i // pairs, i % pairs, side, i // per, i % per) for side in range(2) for i in range(2 * pairs)
    ]


def add_vector(s, which, value):
    for vector, piece, side, chunk, row in vector_slots(value.shape[-1]):
        if vector == which:
            s.vectors[side, chunk, row : row + 1, :] += value[:, pair_lanes(piece)]


def second_norm(s):
    for rows in blocks_of(s, 512):
        ffn = s.total[rows, :]
        ffn_low = ffn.astype(BF16)
        act, slope = gelu_parts(dot(ffn_low, s.down_two[...], NT))
        act = act.astype(BF16)
        normed = s.unit_one[rows, :] * s.gain_one[...] + s.bias_one[...]
        hidden = normed + ffn + dot(act, s.up_two[...])
        unit, inverse = norm_forward(hidden)
        dy = s.cotangent[rows, :].astype(F32)
        s.output[rows, :] = (unit * s.gain_two[...] + s.bias_two[...]).astype(BF16)
        add_vector(s, 2, jnp.sum(dy * unit, axis=0, keepdims=True))
        add_vector(s, 3, jnp.sum(dy, axis=0, keepdims=True))
        dh = norm_backward(dy, unit, inverse, s.gain_two[...])
        da = dh.astype(BF16)
        s.grads[3, :, :] += dot(act, da, TN)
        dz = (dot(da, s.up_two[...], NT) * slope).astype(BF16)
        s.grads[2, :, :] += dot(dz, ffn_low, TN)
        s.total[rows, :] = dh
        s.dffn[rows, :] = (dh + dot(dz, s.down_two[...])).astype(BF16)


def feed_backward(s):
    for tile in range(s.w_inner.shape[0]):
        for rows in blocks_of(s):
            du = dot(s.dffn[rows, :], s.w_outer[tile], NT) * s.slope[tile, rows, :].astype(F32)
            s.total[rows, :] += dot(du.astype(BF16), s.w_inner[tile], NT)


def first_norm_backward(s):
    for rows in [pl.ds(0, s.near_rows), *far_blocks(s)]:
        dy = s.total[rows, :]
        unit = s.unit_one[rows, :]
        add_vector(s, 0, jnp.sum(dy * unit, axis=0, keepdims=True))
        add_vector(s, 1, jnp.sum(dy, axis=0, keepdims=True))
        dh = norm_backward(dy, unit, s.inverse_one[rows, :], s.gain_one[...])
        if rows.start == 0:
            s.near_total[...] = dh
        else:
            s.total[rows, :] = dh
        da = dh.astype(BF16)
        s.grads[1, :, :] += dot(s.act_one[rows, :], da, TN)
        dz = (dot(da, s.up_one[...], NT) * s.slope_one[rows, :]).astype(BF16)
        s.grads[0, :, :] += dot(dz, s.out_low[rows, :], TN)
        dout = (dh + dot(dz, s.down_one[...])).astype(BF16)
        s.ctx[rows, :] = dot(dout, s.w_out[...], NT).astype(BF16)


def project_back(s, total, grads, target):
    weights = (s.w_query, s.w_key, s.w_value)
    rows = target.shape[0]
    for block in [pl.ds(at, min(BLOCK, rows)) for at in range(0, rows, BLOCK)]:
        grad = total[block, :]
        for which, weight in enumerate(weights):
            grad = grad + dot(grads[which, block, :], weight[...], NT)
        target[block, :] = grad.astype(BF16)


INPUTS = (
    "w_query", "w_key", "w_value", "w_out", "w_inner", "w_outer",
    "down_one", "up_one", "down_two", "up_two",
    "gain_one", "bias_one", "gain_two", "bias_two",
)
BIG = INPUTS[:6]


def layer_scratch(span, near, per, width, hidden, adapt):
    pairs, tiles = width // LANES, hidden // width
    v = pltpu.VMEM
    return {
        "v_w_query": v((width, width), BF16),
        "v_w_key": v((width, width), BF16),
        "v_w_value": v((width, width), BF16),
        "v_w_out": v((width, width), BF16),
        "v_w_inner": v((tiles, width, width), BF16),
        "v_w_outer": v((tiles, width, width), BF16),
        "all_query": v((per, pairs, span, LANES), BF16),
        "all_key": v((per, pairs, span, LANES), BF16),
        "all_value": v((per, pairs, span, LANES), BF16),
        "expo": v((2 * pairs, span, span), BF16),
        "inv": v((pairs, span, LANES), F32),
        "attn": v((pairs, span, LANES), F32),
        "ctx": v((span, width), BF16),
        "out_low": v((span, width), BF16),
        "act_one": v((span, adapt), BF16),
        "slope_one": v((span, adapt), F32),
        "unit_one": v((span, width), F32),
        "inverse_one": v((span, 1), F32),
        "normed_low": v((span, width), BF16),
        "slope": v((tiles, span, width), BF16),
        "total": v((span, width), F32),
        "dffn": v((span, width), BF16),
        "all_near_grads": v((per, 3, near, width), BF16),
        "all_near_total": v((per, near, width), F32),
        "far_grads": v((3, span - near, width), BF16),
    }


class Reduce:
    def __init__(self, s, side, parts, devices, me, refs):
        self.s, self.side = s, side
        self.half, self.pair = lax.rem(me, 2), me // 2
        self.pairs, self.outer = parts // 2, devices // GROUP
        place = lax.axis_index("dp")
        self.inner, self.group = lax.rem(place, GROUP), place // GROUP
        self.send, self.got_near, self.part, self.got_dp, self.got_far, self.full, self.sems = (
            ref.at[side] for ref in refs
        )
        self.near = {"seq": me + 1 - 2 * self.half}
        self.ring = [lax.rem(self.inner + k, GROUP) for k in range(GROUP)]
        self.across = [{"dp": self.group * GROUP + k} for k in self.ring]
        self.far = [
            {
                "seq": lax.rem(self.pair + k % self.pairs, self.pairs) * 2 + self.half,
                "dp": lax.rem(self.group + k // self.pairs, self.outer) * GROUP + self.inner,
            }
            for k in range(self.pairs * self.outer)
        ]

    def greeted(self):
        return [self.near, *self.across[1:], *self.far[1:]]

    def copies(self, stage):
        mine, theirs = self.half * GROUP, (1 - self.half) * GROUP
        if stage == 0:
            moves = [(self.send.at[pl.ds(theirs, GROUP)], self.got_near, self.near)]
        elif stage == 1:
            moves = [(self.part.at[self.ring[k]], self.got_dp.at[k], self.across[k]) for k in range(1, GROUP)]
        elif stage == 2:
            block = self.got_far.at[self.group * self.pairs + self.pair]
            moves = [(block, block, device) for device in self.far[1:]]
        elif stage == 3:
            block = self.full.at[mine + self.inner]
            moves = [(block, block, device) for device in self.across[1:]]
        else:
            block = self.full.at[pl.ds(mine, GROUP)]
            moves = [(block, block, self.near)]
        return [
            pltpu.make_async_remote_copy(
                src_ref=source,
                dst_ref=target,
                send_sem=self.sems.at[0, stage, k],
                recv_sem=self.sems.at[1, stage, k],
                device_id=device,
                device_id_type=MESH,
            )
            for k, (source, target, device) in enumerate(moves)
        ]

    def start(self, stage):
        for copy in self.copies(stage):
            copy.start()

    def finish(self, stage):
        for copy in self.copies(stage):
            copy.wait()

    def first(self):
        grads, vectors = self.s.grads, self.s.vectors
        adapt, width = grads.shape[1:]
        chunks, rows = self.send.shape[:2]
        for c in range(chunks):
            at = c * rows
            matrix = 2 * self.side + at // adapt
            self.send[c, :, :width] = grads[matrix, at % adapt : at % adapt + rows, :].astype(BF16)
            self.send[c, :, width:] = vectors[self.side, c].astype(BF16)
        self.start(0)

    def second(self):
        self.finish(0)
        total = self.send[pl.ds(self.half * GROUP, GROUP)].astype(F32) + self.got_near[...].astype(F32)
        self.part[...] = total.astype(BF16)
        self.start(1)

    def third(self):
        self.finish(1)
        total = self.part[self.inner].astype(F32)
        for k in range(1, GROUP):
            total = total + self.got_dp[k].astype(F32)
        self.got_far[self.group * self.pairs + self.pair] = total.astype(BF16)
        self.start(2)

    def fourth(self):
        self.finish(2)
        total = self.got_far[0].astype(F32)
        for k in range(1, self.pairs * self.outer):
            total = total + self.got_far[k].astype(F32)
        self.full[self.half * GROUP + self.inner] = total.astype(BF16)
        self.start(3)

    def fifth(self):
        self.finish(3)
        self.start(4)


def layer_kernel(parts, devices, per, lengths, tokens, cotangent, *refs):
    s = Refs()
    refs = list(refs)
    for name in INPUTS:
        setattr(s, name, refs.pop(0))
    for name in INPUTS[10:]:
        setattr(s, name, getattr(s, name)[...].reshape(1, -1))
    hbm = {name: getattr(s, name) for name in BIG}
    output, grad_in, full = (refs.pop(0) for _ in range(3))
    for name in layer_scratch(LANES, 8, 1, LANES, LANES, 8):
        setattr(s, name, refs.pop(0))
    s.grads, s.vectors, x_in, dy_in = (refs.pop(0) for _ in range(4))
    w_sem, own_sem, send_sem, recv_sem = (refs.pop(0) for _ in range(4))

    me = lax.axis_index("seq")
    rows = tokens.shape[1]
    couples = parts // 2
    core, couple = lax.rem(me, 2), me // 2
    s.near_rows = 2 * rows
    s.shifts = []
    for k in range(couples):
        s.shifts.append((k * 2 * rows, (lax.rem(couple + k, couples) - k) * 2 * rows))
    near = [(0, 1 - core)]
    far = [(k, c) for c in range(2) for k in range(1, couples)]

    def index_of(peer):
        k, c = peer
        return lax.rem(couple + k, couples) * 2 + c

    refs.insert(5, full)
    one, two = (Reduce(s, side, parts, devices, me, refs) for side in range(2))

    barrier = pltpu.get_barrier_semaphore()
    greeted = [{"seq": index_of(peer)} for peer in near + far] + one.greeted()
    for device in greeted:
        pl.semaphore_signal(barrier, inc=1, device_id=device, device_id_type=MESH)

    width = tokens.shape[2]
    weight_copies = []
    for index, name in enumerate(BIG):
        ref = getattr(s, "v_" + name)
        if name == "w_inner":
            for t in range(ref.shape[0]):
                weight_copies.append(
                    pltpu.make_async_copy(hbm[name].at[:, pl.ds(t * width, width)], ref.at[t], w_sem.at[index, t])
                )
        elif name == "w_outer":
            for t in range(ref.shape[0]):
                weight_copies.append(
                    pltpu.make_async_copy(hbm[name].at[pl.ds(t * width, width), :], ref.at[t], w_sem.at[index, t])
                )
        else:
            weight_copies.append(pltpu.make_async_copy(hbm[name], ref, w_sem.at[index, 0]))
        setattr(s, name, ref)

    pl.semaphore_wait(barrier, len(greeted))

    def move(array, step, peer, slot):
        k, c = (0, core) if peer is None else peer
        other = me if peer is None else index_of(peer)
        outside, inside = ((tokens, x_in), (cotangent, dy_in), (output, dy_in), (grad_in, x_in))[array]
        if array < 2:
            source = outside.at[step * parts + other]
            target = inside.at[step, pl.ds((couples - k) % couples * 2 * rows + core * rows, rows)]
        else:
            source = inside.at[step, pl.ds(k * 2 * rows + c * rows, rows)]
            target = outside.at[step * parts + me]
        if peer is None:
            return pltpu.make_async_copy(source, target, own_sem.at[array, step])
        return pltpu.make_async_remote_copy(
            src_ref=source,
            dst_ref=target,
            send_sem=send_sem.at[array, step, other],
            recv_sem=recv_sem.at[array, step, other if slot is None else slot],
            device_id={"seq": other},
            device_id_type=MESH,
        )

    def start(array, step, peers):
        for peer in peers:
            move(array, step, peer, me).start()

    def finish(array, step, peers):
        for peer in peers:
            move(array, step, peer, None).wait()

    near = near + [None]
    everyone = far + near

    def view(step):
        s.tokens, s.cotangent = x_in.at[step], dy_in.at[step]
        s.query, s.key, s.value = (ref.at[step] for ref in (s.all_query, s.all_key, s.all_value))
        s.near_grads, s.near_total = s.all_near_grads.at[step], s.all_near_total.at[step]
        s.output = s.cotangent
        s.length = lengths[step * parts + me]

    near_rows, far_rows = pl.ds(0, s.near_rows), pl.ds(s.near_rows, x_in.shape[1] - s.near_rows)
    start(0, 0, far)
    for step in range(per):
        start(0, step, near)
    for copy in weight_copies:
        copy.start()
    for ref in (s.grads, s.vectors):
        ref[...] = jnp.zeros_like(ref)
    for copy in weight_copies[:3]:
        copy.wait()

    @pl.loop(0, per)
    def _(step):
        view(step)
        finish(0, step, near)
        project_in(s, [near_rows])

    for copy in weight_copies[3:]:
        copy.wait()

    @pl.loop(0, per)
    def _(step):
        more, final = step + 1 < per, step == per - 1
        view(step)
        finish(0, step, far)

        @pl.when(step == 0)
        def _():
            start(1, 0, everyone)

        @pl.when(more)
        def _():
            start(0, step + 1, far)

        project_in(s, far_blocks(s))
        attend_forward(s)
        first_norm(s)
        feed_forward(s)
        finish(1, step, everyone)

        @pl.when(more)
        def _():
            start(1, step + 1, everyone)

        at_end = pl.when(final)
        second_norm(s)
        start(2, step, everyone)
        feed_backward(s)
        first_norm_backward(s)

        @at_end
        def _():
            two.first()
            one.first()
            two.second()
            one.second()

        for pair in range(s.query.shape[0]):
            attend_backward(s, pair)

        @at_end
        def _():
            two.third()
            one.third()

        project_back(s, s.total.at[far_rows], s.far_grads, x_in.at[step, far_rows])
        start(3, step, far)

    for step in range(per):
        view(step)
        project_back(s, s.near_total, s.near_grads, x_in.at[step, near_rows])
        start(3, step, near)
        if step == 0:
            two.fourth()
            one.fourth()
    two.fifth()
    one.fifth()
    one.finish(4)
    two.finish(4)

    @pl.loop(0, per)
    def _(step):
        finish(2, step, everyone)
        finish(3, step, everyone)


def tail_kernel(output, grad_in, full, output_out, grad_in_out, *grads):
    output_out[...] = output[...]
    grad_in_out[...] = grad_in[...].astype(F32)

    @pl.when(pl.program_id(0) == 0)
    def _():
        matrices, vectors = grads[:4], grads[4:]
        adapt, width = matrices[0].shape
        chunks, rows = full.shape[1:3]
        for side in range(2):
            for c in range(chunks):
                at = c * rows
                matrix = matrices[2 * side + at // adapt]
                matrix[at % adapt : at % adapt + rows, :] = full[side, c, :, :width].astype(F32)
        tails = full[:, :, :, width:].astype(F32)
        for vector, piece, side, chunk, row in vector_slots(width):
            vectors[vector][pair_lanes(piece)] = tails[side, chunk, row]


def per_device(parts, devices, tokens, lengths, cotangent, *params):
    batch, rows, width = tokens.shape
    hidden, adapt = params[4].shape[1], params[6].shape[1]
    per, span = batch // parts, parts * rows
    chunks, chunk_rows = 2 * GROUP, adapt // GROUP
    far = parts // 2 * (devices // GROUP)
    params = list(params)
    params[6], params[8] = params[6].T, params[8].T
    vmem = pl.BlockSpec(memory_space=pltpu.VMEM)
    anywhere = pl.BlockSpec(memory_space=pl.ANY)
    dma = pltpu.SemaphoreType.DMA
    chunk = (chunk_rows, width + LANES)
    scratch = [
        *layer_scratch(span, 2 * rows, per, width, hidden, adapt).values(),
        pltpu.VMEM((4, adapt, width), F32),
        pltpu.VMEM((2, chunks, chunk_rows, LANES), F32),
        *[pltpu.VMEM((per, span, width), BF16)] * 2,
        dma((len(BIG), hidden // width)),
        dma((4, per)),
        dma((4, per, parts)),
        dma((4, per, parts)),
        pltpu.VMEM((2, chunks, *chunk), BF16),
        *[pltpu.VMEM((2, GROUP, *chunk), BF16)] * 3,
        pltpu.VMEM((2, far, *chunk), BF16),
        dma((2, 2, 5, max(GROUP, far))),
    ]
    moved = jax.ShapeDtypeStruct((batch, rows, width), BF16)
    summed = jax.ShapeDtypeStruct((2, chunks, *chunk), BF16)
    output, grad_in, full = pl.pallas_call(
        functools.partial(layer_kernel, parts, devices, per),
        out_shape=(moved, moved, summed),
        in_specs=[pl.BlockSpec(memory_space=pltpu.SMEM)]
        + [anywhere] * 2
        + [anywhere if name in BIG else vmem for name in INPUTS],
        out_specs=(anywhere, anywhere, vmem),
        scratch_shapes=scratch,
        compiler_params=pltpu.CompilerParams(
            collective_id=0, has_side_effects=True, vmem_limit_bytes=62 * 2**20
        ),
        name="layer",
    )(lengths, tokens, cotangent, *params)
    block = pl.BlockSpec((batch // 2, rows, width), lambda i: (i, 0, 0))
    whole = [pl.BlockSpec((adapt, width), lambda i: (0, 0))] * 4 + [pl.BlockSpec((width,), lambda i: (0,))] * 4
    output, grad_in, down_one, up_one, down_two, up_two, *vectors = pl.pallas_call(
        tail_kernel,
        grid=(2,),
        out_shape=(
            moved,
            jax.ShapeDtypeStruct((batch, rows, width), F32),
            *[jax.ShapeDtypeStruct((adapt, width), F32)] * 4,
            *[jax.ShapeDtypeStruct((width,), F32)] * 4,
        ),
        in_specs=[block, block, pl.BlockSpec(summed.shape, lambda i: (0, 0, 0, 0))],
        out_specs=(block, block, *whole),
        name="tail",
    )(output, grad_in, full)
    return (output, grad_in, down_one.T, up_one, down_two.T, up_two, *vectors)


def solution(mesh):
    split = P("dp", "seq", None)
    return jax.shard_map(
        functools.partial(per_device, mesh.shape["seq"], mesh.shape["dp"]),
        mesh=mesh,
        in_specs=(split, P("dp"), split) + (P(),) * 14,
        out_specs=(split, split) + (P(),) * 8,
        check_vma=False,
    )
```

```python
import functools

import jax
import jax.numpy as jnp
from jax import lax
from jax.experimental import pallas as pl
from jax.experimental.pallas import tpu as pltpu
from jax.sharding import PartitionSpec as P

HEADS = 12
EPS = 1e-06
F32 = jnp.float32
BF16 = jnp.bfloat16
NN = (((1,), (0,)), ((), ()))
NT = (((1,), (1,)), ((), ()))
TN = (((0,), (0,)), ((), ()))
MESH = pl.DeviceIdType.MESH
LANES = 128
GROUP = 8


def dot(left, right, dims=NN):
    return lax.dot_general(left, right, dims, preferred_element_type=F32)


def gelu_parts(value):
    phi = 0.5 + 0.5 * lax.erf(value * 0.7071067811865476)
    scaled = value * jnp.exp(value * value * -0.5) * 0.3989422804014327
    return value * phi, phi + scaled


def row_mean(value):
    return jnp.sum(value, axis=-1, keepdims=True) * (1.0 / value.shape[-1])


def norm_forward(hidden):
    centred = hidden - row_mean(hidden)
    inverse = lax.rsqrt(row_mean(centred * centred) + EPS)
    return centred * inverse, inverse


def norm_backward(grad, unit, inverse, gain):
    scaled = grad * gain
    inner = scaled - row_mean(scaled) - unit * row_mean(scaled * unit)
    return inner * inverse


class Refs:
    pass


def pair_lanes(pair):
    return slice(pair * LANES, (pair + 1) * LANES)


def attend_forward(s):
    pairs, span = s.query.shape[:2]
    low = lax.broadcasted_iota(jnp.int32, (1, LANES), 1) < LANES // 2
    column = lax.broadcasted_iota(jnp.int32, (1, span), 1)
    position = column
    for at, shift in s.shifts:
        position = jnp.where(column >= at, column + shift, position)
    bias = jnp.where(position < s.length, 0.0, -1e30)
    for pair in range(pairs):
        key, value = s.key[pair], s.value[pair]
        zero = jnp.zeros_like(key)
        keys = (jnp.where(low, key, zero), jnp.where(low, zero, key))
        value = jnp.concatenate([value, jnp.ones_like(value)], axis=1)
        for rows in blocks_of(s):
            query = s.query[pair, rows, :]
            outs, totals = [], []
            for head in range(2):
                scores = dot(query, keys[head], NT) + bias
                expo = jnp.exp(scores - jnp.max(scores, axis=-1, keepdims=True)).astype(BF16)
                s.expo[2 * pair + head, rows, :] = expo
                product = dot(expo, value)
                outs.append(product[:, :LANES])
                totals.append(product[:, LANES:])
            inv = 1.0 / jnp.where(low, *totals)
            attn = jnp.where(low, *outs) * inv
            s.inv[pair, rows, :] = inv
            s.attn[pair, rows, :] = attn
            s.ctx[rows, pair_lanes(pair)] = attn.astype(BF16)


def attend_backward(s, pair):
    low = lax.broadcasted_iota(jnp.int32, (1, LANES), 1) < LANES // 2
    lanes = pair_lanes(pair)
    key, value, query = s.key[pair], s.value[pair], s.query[pair]
    zero = jnp.zeros_like(key)
    wide = s.ctx[:, lanes].astype(F32) * s.inv[pair]
    terms = wide * s.attn[pair]
    grad = wide.astype(BF16)
    grad_t, query_t = grad.T, query.T
    dquery, dkey, dvalue = 0.0, [], []
    for head in range(2):
        mine = low if head == 0 else ~low
        sub = slice(head * LANES // 2, (head + 1) * LANES // 2)
        delta = jnp.sum(jnp.where(mine, terms, 0.0), axis=-1, keepdims=True)
        expo = s.expo[2 * pair + head]
        dprob = dot(jnp.where(mine, grad, zero), value, NT)
        dscores = (expo.astype(F32) * (dprob - delta)).astype(BF16)
        dquery = dquery + dot(dscores, jnp.where(mine, key, zero))
        dvalue.append(dot(grad_t[sub], expo).astype(BF16))
        dkey.append(dot(query_t[sub], dscores).astype(BF16))
    grads = (
        (dquery * (LANES // 2) ** -0.5).astype(BF16),
        jnp.concatenate(dkey, axis=0).T,
        jnp.concatenate(dvalue, axis=0).T,
    )
    for which, grad in enumerate(grads):
        s.near_grads[which, :, lanes] = grad[: s.near_rows]
        s.far_grads[which, :, lanes] = grad[s.near_rows :]


BLOCK = 256


def blocks_of(s, block=BLOCK):
    return [pl.ds(b * block, block) for b in range(s.tokens.shape[0] // block)]


def far_blocks(s):
    near, span = s.near_rows, s.tokens.shape[0]
    return [pl.ds(at, BLOCK) for at in range(near, span, BLOCK)]


def project_in(s, blocks):
    pairs = s.query.shape[0]
    scale = jnp.asarray((LANES // 2) ** -0.5, BF16)
    for rows in blocks:
        x = s.tokens[rows, :]
        for weight, target in ((s.w_query, s.query), (s.w_key, s.key), (s.w_value, s.value)):
            y = dot(x, weight[...]).astype(BF16)
            if target is s.query:
                y = y * scale
            for pair in range(pairs):
                target[pair, rows, :] = y[:, pair * LANES : (pair + 1) * LANES]


def first_norm(s):
    for rows in blocks_of(s, 512):
        out = dot(s.ctx[rows, :], s.w_out[...])
        out_low = out.astype(BF16)
        s.out_low[rows, :] = out_low
        act, slope = gelu_parts(dot(out_low, s.down_one[...], NT))
        act = act.astype(BF16)
        s.act_one[rows, :] = act
        s.slope_one[rows, :] = slope
        hidden = s.tokens[rows, :].astype(F32) + out + dot(act, s.up_one[...])
        unit, inverse = norm_forward(hidden)
        s.unit_one[rows, :] = unit
        s.inverse_one[rows, :] = inverse
        normed = unit * s.gain_one[...] + s.bias_one[...]
        s.normed_low[rows, :] = normed.astype(BF16)
        s.total[rows, :] = jnp.zeros_like(normed)


def feed_forward(s):
    for tile in range(s.w_inner.shape[0]):
        for rows in blocks_of(s):
            act, slope = gelu_parts(dot(s.normed_low[rows, :], s.w_inner[tile]))
            s.slope[tile, rows, :] = slope.astype(BF16)
            s.total[rows, :] += dot(act.astype(BF16), s.w_outer[tile])


def vector_slots(width):
    pairs = width // LANES
    per = pl.cdiv(2 * pairs, 2 * GROUP)
    return [
        (2 * side + i // pairs, i % pairs, side, i // per, i % per) for side in range(2) for i in range(2 * pairs)
    ]


def add_vector(s, which, value):
    for vector, piece, side, chunk, row in vector_slots(value.shape[-1]):
        if vector == which:
            s.vectors[side, chunk, row : row + 1, :] += value[:, pair_lanes(piece)]


def lockstep(stages):
    stages = list(stages)
    while stages:
        for stage in list(stages):
            try:
                next(stage)
            except StopIteration:
                stages.remove(stage)


def second_norm(s, rows):
    ffn = s.total[rows, :]
    ffn_low = ffn.astype(BF16)
    zed = dot(ffn_low, s.down_two[...], NT)
    yield
    act, slope = gelu_parts(zed)
    act = act.astype(BF16)
    branch = dot(act, s.up_two[...])
    yield
    normed = s.unit_one[rows, :] * s.gain_one[...] + s.bias_one[...]
    unit, inverse = norm_forward(normed + ffn + branch)
    dy = s.cotangent[rows, :].astype(F32)
    s.output[rows, :] = (unit * s.gain_two[...] + s.bias_two[...]).astype(BF16)
    add_vector(s, 2, jnp.sum(dy * unit, axis=0, keepdims=True))
    add_vector(s, 3, jnp.sum(dy, axis=0, keepdims=True))
    dh = norm_backward(dy, unit, inverse, s.gain_two[...])
    s.total[rows, :] = dh
    da = dh.astype(BF16)
    yield
    back = dot(da, s.up_two[...], NT)
    s.grads[3, :, :] += dot(act, da, TN)
    yield
    dz = (back * slope).astype(BF16)
    s.dffn[rows, :] = (dh + dot(dz, s.down_two[...])).astype(BF16)
    s.grads[2, :, :] += dot(dz, ffn_low, TN)


def feed_backward(s):
    for tile in range(s.w_inner.shape[0]):
        for rows in blocks_of(s):
            du = dot(s.dffn[rows, :], s.w_outer[tile], NT) * s.slope[tile, rows, :].astype(F32)
            s.total[rows, :] += dot(du.astype(BF16), s.w_inner[tile], NT)


def first_norm_backward(s, rows):
    dy = s.total[rows, :]
    unit = s.unit_one[rows, :]
    add_vector(s, 0, jnp.sum(dy * unit, axis=0, keepdims=True))
    add_vector(s, 1, jnp.sum(dy, axis=0, keepdims=True))
    dh = norm_backward(dy, unit, s.inverse_one[rows, :], s.gain_one[...])
    if rows.start == 0:
        s.near_total[...] = dh
    else:
        s.total[rows, :] = dh
    da = dh.astype(BF16)
    yield
    back = dot(da, s.up_one[...], NT)
    s.grads[1, :, :] += dot(s.act_one[rows, :], da, TN)
    yield
    dz = (back * s.slope_one[rows, :]).astype(BF16)
    branch = dot(dz, s.down_one[...])
    s.grads[0, :, :] += dot(dz, s.out_low[rows, :], TN)
    yield
    dout = (dh + branch).astype(BF16)
    s.ctx[rows, :] = dot(dout, s.w_out[...], NT).astype(BF16)


def project_back(s, total, grads, target):
    weights = (s.w_query, s.w_key, s.w_value)
    rows = target.shape[0]
    for block in [pl.ds(at, min(BLOCK, rows)) for at in range(0, rows, BLOCK)]:
        grad = total[block, :]
        for which, weight in enumerate(weights):
            grad = grad + dot(grads[which, block, :], weight[...], NT)
        target[block, :] = grad.astype(BF16)


INPUTS = (
    "w_query", "w_key", "w_value", "w_out", "w_inner", "w_outer",
    "down_one", "up_one", "down_two", "up_two",
    "gain_one", "bias_one", "gain_two", "bias_two",
)
BIG = INPUTS[:6]


def layer_scratch(span, near, per, width, hidden, adapt):
    pairs, tiles = width // LANES, hidden // width
    v = pltpu.VMEM
    return {
        "v_w_query": v((width, width), BF16),
        "v_w_key": v((width, width), BF16),
        "v_w_value": v((width, width), BF16),
        "v_w_out": v((width, width), BF16),
        "v_w_inner": v((tiles, width, width), BF16),
        "v_w_outer": v((tiles, width, width), BF16),
        "all_query": v((per, pairs, span, LANES), BF16),
        "all_key": v((per, pairs, span, LANES), BF16),
        "all_value": v((per, pairs, span, LANES), BF16),
        "expo": v((2 * pairs, span, span), BF16),
        "inv": v((pairs, span, LANES), F32),
        "attn": v((pairs, span, LANES), F32),
        "ctx": v((span, width), BF16),
        "out_low": v((span, width), BF16),
        "act_one": v((span, adapt), BF16),
        "slope_one": v((span, adapt), F32),
        "unit_one": v((span, width), F32),
        "inverse_one": v((span, 1), F32),
        "normed_low": v((span, width), BF16),
        "slope": v((tiles, span, width), BF16),
        "total": v((span, width), F32),
        "dffn": v((span, width), BF16),
        "all_near_grads": v((per, 3, near, width), BF16),
        "all_near_total": v((per, near, width), F32),
        "far_grads": v((3, span - near, width), BF16),
    }


class Reduce:
    def __init__(self, s, side, parts, devices, me, refs):
        self.s, self.side = s, side
        self.half, self.pair = lax.rem(me, 2), me // 2
        self.pairs, self.outer = parts // 2, devices // GROUP
        place = lax.axis_index("dp")
        self.inner, self.group = lax.rem(place, GROUP), place // GROUP
        self.send, self.got_near, self.part, self.got_dp, self.got_far, self.full, self.sems = (
            ref.at[side] for ref in refs
        )
        self.near = {"seq": me + 1 - 2 * self.half}
        self.ring = [lax.rem(self.inner + k, GROUP) for k in range(GROUP)]
        self.across = [{"dp": self.group * GROUP + k} for k in self.ring]
        self.far = [
            {
                "seq": lax.rem(self.pair + k % self.pairs, self.pairs) * 2 + self.half,
                "dp": lax.rem(self.group + k // self.pairs, self.outer) * GROUP + self.inner,
            }
            for k in range(self.pairs * self.outer)
        ]

    def greeted(self):
        return [self.near, *self.across[1:], *self.far[1:]]

    def copies(self, stage):
        mine, theirs = self.half * GROUP, (1 - self.half) * GROUP
        if stage == 0:
            moves = [(self.send.at[pl.ds(theirs, GROUP)], self.got_near, self.near)]
        elif stage == 1:
            moves = [(self.part.at[self.ring[k]], self.got_dp.at[k], self.across[k]) for k in range(1, GROUP)]
        elif stage == 2:
            block = self.got_far.at[self.group * self.pairs + self.pair]
            moves = [(block, block, device) for device in self.far[1:]]
        elif stage == 3:
            block = self.full.at[mine + self.inner]
            moves = [(block, block, device) for device in self.across[1:]]
        else:
            block = self.full.at[pl.ds(mine, GROUP)]
            moves = [(block, block, self.near)]
        return [
            pltpu.make_async_remote_copy(
                src_ref=source,
                dst_ref=target,
                send_sem=self.sems.at[0, stage, k],
                recv_sem=self.sems.at[1, stage, k],
                device_id=device,
                device_id_type=MESH,
            )
            for k, (source, target, device) in enumerate(moves)
        ]

    def start(self, stage):
        for copy in self.copies(stage):
            copy.start()

    def finish(self, stage):
        for copy in self.copies(stage):
            copy.wait()

    def first(self):
        grads, vectors = self.s.grads, self.s.vectors
        adapt, width = grads.shape[1:]
        chunks, rows = self.send.shape[:2]
        for c in range(chunks):
            at = c * rows
            matrix = 2 * self.side + at // adapt
            self.send[c, :, :width] = grads[matrix, at % adapt : at % adapt + rows, :].astype(BF16)
            self.send[c, :, width:] = vectors[self.side, c].astype(BF16)
        self.start(0)

    def second(self):
        self.finish(0)
        total = self.send[pl.ds(self.half * GROUP, GROUP)].astype(F32) + self.got_near[...].astype(F32)
        self.part[...] = total.astype(BF16)
        self.start(1)

    def third(self):
        self.finish(1)
        total = self.part[self.inner].astype(F32)
        for k in range(1, GROUP):
            total = total + self.got_dp[k].astype(F32)
        self.got_far[self.group * self.pairs + self.pair] = total.astype(BF16)
        self.start(2)

    def fourth(self):
        self.finish(2)
        total = self.got_far[0].astype(F32)
        for k in range(1, self.pairs * self.outer):
            total = total + self.got_far[k].astype(F32)
        self.full[self.half * GROUP + self.inner] = total.astype(BF16)
        self.start(3)

    def fifth(self):
        self.finish(3)
        self.start(4)


def layer_kernel(parts, devices, per, lengths, tokens, cotangent, *refs):
    s = Refs()
    refs = list(refs)
    for name in INPUTS:
        setattr(s, name, refs.pop(0))
    for name in INPUTS[10:]:
        setattr(s, name, getattr(s, name)[...].reshape(1, -1))
    hbm = {name: getattr(s, name) for name in BIG}
    output, grad_in, full = (refs.pop(0) for _ in range(3))
    for name in layer_scratch(LANES, 8, 1, LANES, LANES, 8):
        setattr(s, name, refs.pop(0))
    s.grads, s.vectors, x_in, dy_in = (refs.pop(0) for _ in range(4))
    w_sem, own_sem, send_sem, recv_sem = (refs.pop(0) for _ in range(4))

    me = lax.axis_index("seq")
    rows = tokens.shape[1]
    couples = parts // 2
    core, couple = lax.rem(me, 2), me // 2
    s.near_rows = 2 * rows
    s.shifts = []
    for k in range(couples):
        s.shifts.append((k * 2 * rows, (lax.rem(couple + k, couples) - k) * 2 * rows))
    near = [(0, 1 - core)]
    far = [(k, c) for c in range(2) for k in range(1, couples)]

    def index_of(peer):
        k, c = peer
        return lax.rem(couple + k, couples) * 2 + c

    refs.insert(5, full)
    one, two = (Reduce(s, side, parts, devices, me, refs) for side in range(2))

    barrier = pltpu.get_barrier_semaphore()
    greeted = [{"seq": index_of(peer)} for peer in near + far] + one.greeted()
    for device in greeted:
        pl.semaphore_signal(barrier, inc=1, device_id=device, device_id_type=MESH)

    width = tokens.shape[2]
    weight_copies = []
    for index, name in enumerate(BIG):
        ref = getattr(s, "v_" + name)
        if name == "w_inner":
            for t in range(ref.shape[0]):
                weight_copies.append(
                    pltpu.make_async_copy(hbm[name].at[:, pl.ds(t * width, width)], ref.at[t], w_sem.at[index, t])
                )
        elif name == "w_outer":
            for t in range(ref.shape[0]):
                weight_copies.append(
                    pltpu.make_async_copy(hbm[name].at[pl.ds(t * width, width), :], ref.at[t], w_sem.at[index, t])
                )
        else:
            weight_copies.append(pltpu.make_async_copy(hbm[name], ref, w_sem.at[index, 0]))
        setattr(s, name, ref)

    pl.semaphore_wait(barrier, len(greeted))

    def move(array, step, peer, slot):
        k, c = (0, core) if peer is None else peer
        other = me if peer is None else index_of(peer)
        outside, inside = ((tokens, x_in), (cotangent, dy_in), (output, dy_in), (grad_in, x_in))[array]
        if array < 2:
            source = outside.at[step * parts + other]
            target = inside.at[step, pl.ds((couples - k) % couples * 2 * rows + core * rows, rows)]
        else:
            source = inside.at[step, pl.ds(k * 2 * rows + c * rows, rows)]
            target = outside.at[step * parts + me]
        if peer is None:
            return pltpu.make_async_copy(source, target, own_sem.at[array, step])
        return pltpu.make_async_remote_copy(
            src_ref=source,
            dst_ref=target,
            send_sem=send_sem.at[array, step, other],
            recv_sem=recv_sem.at[array, step, other if slot is None else slot],
            device_id={"seq": other},
            device_id_type=MESH,
        )

    def start(array, step, peers):
        for peer in peers:
            move(array, step, peer, me).start()

    def finish(array, step, peers):
        for peer in peers:
            move(array, step, peer, None).wait()

    near = near + [None]
    everyone = far + near

    def view(step):
        s.tokens, s.cotangent = x_in.at[step], dy_in.at[step]
        s.query, s.key, s.value = (ref.at[step] for ref in (s.all_query, s.all_key, s.all_value))
        s.near_grads, s.near_total = s.all_near_grads.at[step], s.all_near_total.at[step]
        s.output = s.cotangent
        s.length = lengths[step * parts + me]

    near_rows, far_rows = pl.ds(0, s.near_rows), pl.ds(s.near_rows, x_in.shape[1] - s.near_rows)
    start(0, 0, far)
    for step in range(per):
        start(0, step, near)
    for copy in weight_copies:
        copy.start()
    for ref in (s.grads, s.vectors):
        ref[...] = jnp.zeros_like(ref)
    for copy in weight_copies[:3]:
        copy.wait()

    @pl.loop(0, per)
    def _(step):
        view(step)
        finish(0, step, near)
        project_in(s, [near_rows])

    for copy in weight_copies[3:]:
        copy.wait()

    @pl.loop(0, per)
    def _(step):
        more, final = step + 1 < per, step == per - 1
        view(step)
        finish(0, step, far)

        @pl.when(step == 0)
        def _():
            start(1, 0, everyone)

        @pl.when(more)
        def _():
            start(0, step + 1, far)

        project_in(s, far_blocks(s))
        attend_forward(s)
        first_norm(s)
        feed_forward(s)
        finish(1, step, everyone)

        @pl.when(more)
        def _():
            start(1, step + 1, everyone)

        at_end = pl.when(final)
        lockstep(second_norm(s, block) for block in blocks_of(s))
        start(2, step, everyone)
        feed_backward(s)
        lockstep(first_norm_backward(s, block) for block in [near_rows, *far_blocks(s)])

        @at_end
        def _():
            two.first()
            one.first()
            two.second()
            one.second()

        for pair in range(s.query.shape[0]):
            attend_backward(s, pair)

        @at_end
        def _():
            two.third()
            one.third()

        project_back(s, s.total.at[far_rows], s.far_grads, x_in.at[step, far_rows])
        start(3, step, far)

    for step in range(per):
        view(step)
        project_back(s, s.near_total, s.near_grads, x_in.at[step, near_rows])
        start(3, step, near)
        if step == 0:
            two.fourth()
            one.fourth()
    two.fifth()
    one.fifth()
    one.finish(4)
    two.finish(4)

    @pl.loop(0, per)
    def _(step):
        finish(2, step, everyone)
        finish(3, step, everyone)


def tail_kernel(output, grad_in, full, output_out, grad_in_out, *grads):
    output_out[...] = output[...]
    grad_in_out[...] = grad_in[...].astype(F32)

    @pl.when(pl.program_id(0) == 0)
    def _():
        matrices, vectors = grads[:4], grads[4:]
        adapt, width = matrices[0].shape
        chunks, rows = full.shape[1:3]
        for side in range(2):
            for c in range(chunks):
                at = c * rows
                matrix = matrices[2 * side + at // adapt]
                matrix[at % adapt : at % adapt + rows, :] = full[side, c, :, :width].astype(F32)
        tails = full[:, :, :, width:].astype(F32)
        for vector, piece, side, chunk, row in vector_slots(width):
            vectors[vector][pair_lanes(piece)] = tails[side, chunk, row]


def per_device(parts, devices, tokens, lengths, cotangent, *params):
    batch, rows, width = tokens.shape
    hidden, adapt = params[4].shape[1], params[6].shape[1]
    per, span = batch // parts, parts * rows
    chunks, chunk_rows = 2 * GROUP, adapt // GROUP
    far = parts // 2 * (devices // GROUP)
    params = list(params)
    params[6], params[8] = params[6].T, params[8].T
    vmem = pl.BlockSpec(memory_space=pltpu.VMEM)
    anywhere = pl.BlockSpec(memory_space=pl.ANY)
    dma = pltpu.SemaphoreType.DMA
    chunk = (chunk_rows, width + LANES)
    scratch = [
        *layer_scratch(span, 2 * rows, per, width, hidden, adapt).values(),
        pltpu.VMEM((4, adapt, width), F32),
        pltpu.VMEM((2, chunks, chunk_rows, LANES), F32),
        *[pltpu.VMEM((per, span, width), BF16)] * 2,
        dma((len(BIG), hidden // width)),
        dma((4, per)),
        dma((4, per, parts)),
        dma((4, per, parts)),
        pltpu.VMEM((2, chunks, *chunk), BF16),
        *[pltpu.VMEM((2, GROUP, *chunk), BF16)] * 3,
        pltpu.VMEM((2, far, *chunk), BF16),
        dma((2, 2, 5, max(GROUP, far))),
    ]
    moved = jax.ShapeDtypeStruct((batch, rows, width), BF16)
    summed = jax.ShapeDtypeStruct((2, chunks, *chunk), BF16)
    output, grad_in, full = pl.pallas_call(
        functools.partial(layer_kernel, parts, devices, per),
        out_shape=(moved, moved, summed),
        in_specs=[pl.BlockSpec(memory_space=pltpu.SMEM)]
        + [anywhere] * 2
        + [anywhere if name in BIG else vmem for name in INPUTS],
        out_specs=(anywhere, anywhere, vmem),
        scratch_shapes=scratch,
        compiler_params=pltpu.CompilerParams(
            collective_id=0, has_side_effects=True, vmem_limit_bytes=62 * 2**20
        ),
        name="layer",
    )(lengths, tokens, cotangent, *params)
    block = pl.BlockSpec((batch // 2, rows, width), lambda i: (i, 0, 0))
    whole = [pl.BlockSpec((adapt, width), lambda i: (0, 0))] * 4 + [pl.BlockSpec((width,), lambda i: (0,))] * 4
    output, grad_in, down_one, up_one, down_two, up_two, *vectors = pl.pallas_call(
        tail_kernel,
        grid=(2,),
        out_shape=(
            moved,
            jax.ShapeDtypeStruct((batch, rows, width), F32),
            *[jax.ShapeDtypeStruct((adapt, width), F32)] * 4,
            *[jax.ShapeDtypeStruct((width,), F32)] * 4,
        ),
        in_specs=[block, block, pl.BlockSpec(summed.shape, lambda i: (0, 0, 0, 0))],
        out_specs=(block, block, *whole),
        name="tail",
    )(output, grad_in, full)
    return (output, grad_in, down_one.T, up_one, down_two.T, up_two, *vectors)


def solution(mesh):
    split = P("dp", "seq", None)
    return jax.shard_map(
        functools.partial(per_device, mesh.shape["seq"], mesh.shape["dp"]),
        mesh=mesh,
        in_specs=(split, P("dp"), split) + (P(),) * 14,
        out_specs=(split, split) + (P(),) * 8,
        check_vma=False,
    )
```

```python
import functools

import jax
import jax.numpy as jnp
from jax import lax
from jax.experimental import pallas as pl
from jax.experimental.pallas import tpu as pltpu
from jax.sharding import PartitionSpec as P

HEADS = 12
EPS = 1e-06
F32 = jnp.float32
BF16 = jnp.bfloat16
NN = (((1,), (0,)), ((), ()))
NT = (((1,), (1,)), ((), ()))
TN = (((0,), (0,)), ((), ()))
MESH = pl.DeviceIdType.MESH
LANES = 128
GROUP = 8


def dot(left, right, dims=NN):
    return lax.dot_general(left, right, dims, preferred_element_type=F32)


def gelu_parts(value):
    phi = 0.5 + 0.5 * lax.erf(value * 0.7071067811865476)
    scaled = value * jnp.exp(value * value * -0.5) * 0.3989422804014327
    return value * phi, phi + scaled


def row_mean(value):
    return jnp.sum(value, axis=-1, keepdims=True) * (1.0 / value.shape[-1])


def norm_forward(hidden):
    centred = hidden - row_mean(hidden)
    inverse = lax.rsqrt(row_mean(centred * centred) + EPS)
    return centred * inverse, inverse


def norm_backward(grad, unit, inverse, gain):
    scaled = grad * gain
    inner = scaled - row_mean(scaled) - unit * row_mean(scaled * unit)
    return inner * inverse


class Refs:
    pass


def pair_lanes(pair):
    return slice(pair * LANES, (pair + 1) * LANES)


def attend_forward(s):
    pairs, span = s.query.shape[:2]
    low = lax.broadcasted_iota(jnp.int32, (1, LANES), 1) < LANES // 2
    column = lax.broadcasted_iota(jnp.int32, (1, span), 1)
    position = column
    for at, shift in s.shifts:
        position = jnp.where(column >= at, column + shift, position)
    bias = jnp.where(position < s.length, 0.0, -1e30)
    for pair in range(pairs):
        key, value = s.key[pair], s.value[pair]
        zero = jnp.zeros_like(key)
        keys = (jnp.where(low, key, zero), jnp.where(low, zero, key))
        value = jnp.concatenate([value, jnp.ones_like(value)], axis=1)
        for rows in blocks_of(s):
            query = s.query[pair, rows, :]
            outs, totals = [], []
            for head in range(2):
                scores = dot(query, keys[head], NT) + bias
                expo = jnp.exp(scores - jnp.max(scores, axis=-1, keepdims=True)).astype(BF16)
                s.expo[2 * pair + head, rows, :] = expo
                product = dot(expo, value)
                outs.append(product[:, :LANES])
                totals.append(product[:, LANES:])
            inv = 1.0 / jnp.where(low, *totals)
            attn = jnp.where(low, *outs) * inv
            s.inv[pair, rows, :] = inv
            s.attn[pair, rows, :] = attn
            s.ctx[rows, pair_lanes(pair)] = attn.astype(BF16)


def attend_backward(s, pair):
    low = lax.broadcasted_iota(jnp.int32, (1, LANES), 1) < LANES // 2
    lanes = pair_lanes(pair)
    key, value, query = s.key[pair], s.value[pair], s.query[pair]
    zero = jnp.zeros_like(key)
    wide = s.ctx[:, lanes].astype(F32) * s.inv[pair]
    terms = wide * s.attn[pair]
    grad = wide.astype(BF16)
    grad_t, query_t = grad.T, query.T
    dquery, dkey, dvalue = 0.0, [], []
    for head in range(2):
        mine = low if head == 0 else ~low
        sub = slice(head * LANES // 2, (head + 1) * LANES // 2)
        delta = jnp.sum(jnp.where(mine, terms, 0.0), axis=-1, keepdims=True)
        expo = s.expo[2 * pair + head]
        dprob = dot(jnp.where(mine, grad, zero), value, NT)
        dscores = (expo.astype(F32) * (dprob - delta)).astype(BF16)
        dquery = dquery + dot(dscores, jnp.where(mine, key, zero))
        dvalue.append(dot(grad_t[sub], expo).astype(BF16))
        dkey.append(dot(query_t[sub], dscores).astype(BF16))
    grads = (
        (dquery * (LANES // 2) ** -0.5).astype(BF16),
        jnp.concatenate(dkey, axis=0).T,
        jnp.concatenate(dvalue, axis=0).T,
    )
    for which, grad in enumerate(grads):
        s.near_grads[which, :, lanes] = grad[: s.near_rows]
        s.far_grads[which, :, lanes] = grad[s.near_rows :]


BLOCK = 256


def blocks_of(s, block=BLOCK):
    return [pl.ds(b * block, block) for b in range(s.tokens.shape[0] // block)]


def far_blocks(s):
    near, span = s.near_rows, s.tokens.shape[0]
    return [pl.ds(at, BLOCK) for at in range(near, span, BLOCK)]


def project_in(s, blocks):
    pairs = s.query.shape[0]
    scale = jnp.asarray((LANES // 2) ** -0.5, BF16)
    for rows in blocks:
        x = s.tokens[rows, :]
        for weight, target in ((s.w_query, s.query), (s.w_key, s.key), (s.w_value, s.value)):
            y = dot(x, weight[...]).astype(BF16)
            if target is s.query:
                y = y * scale
            for pair in range(pairs):
                target[pair, rows, :] = y[:, pair * LANES : (pair + 1) * LANES]


def first_norm(s):
    for rows in blocks_of(s, 512):
        out = dot(s.ctx[rows, :], s.w_out[...])
        out_low = out.astype(BF16)
        s.out_low[rows, :] = out_low
        act, slope = gelu_parts(dot(out_low, s.down_one[...], NT))
        act = act.astype(BF16)
        s.act_one[rows, :] = act
        s.slope_one[rows, :] = slope
        hidden = s.tokens[rows, :].astype(F32) + out + dot(act, s.up_one[...])
        unit, inverse = norm_forward(hidden)
        s.unit_one[rows, :] = unit
        s.inverse_one[rows, :] = inverse
        normed = unit * s.gain_one[...] + s.bias_one[...]
        s.normed_low[rows, :] = normed.astype(BF16)
        s.total[rows, :] = jnp.zeros_like(normed)


def feed_forward(s):
    for tile in range(s.w_inner.shape[0]):
        for rows in blocks_of(s):
            act, slope = gelu_parts(dot(s.normed_low[rows, :], s.w_inner[tile]))
            s.slope[tile, rows, :] = slope.astype(BF16)
            s.total[rows, :] += dot(act.astype(BF16), s.w_outer[tile])


def vector_slots(width):
    pairs = width // LANES
    per = pl.cdiv(2 * pairs, 2 * GROUP)
    return [
        (2 * side + i // pairs, i % pairs, side, i // per, i % per) for side in range(2) for i in range(2 * pairs)
    ]


def add_vector(s, which, value):
    for vector, piece, side, chunk, row in vector_slots(value.shape[-1]):
        if vector == which:
            s.vectors[side, chunk, row : row + 1, :] += value[:, pair_lanes(piece)]


def lockstep(stages):
    stages = list(stages)
    while stages:
        for stage in list(stages):
            try:
                next(stage)
            except StopIteration:
                stages.remove(stage)


def second_norm(s, rows):
    ffn = s.total[rows, :]
    ffn_low = ffn.astype(BF16)
    zed = dot(ffn_low, s.down_two[...], NT)
    yield
    act, slope = gelu_parts(zed)
    act = act.astype(BF16)
    branch = dot(act, s.up_two[...])
    yield
    normed = s.unit_one[rows, :] * s.gain_one[...] + s.bias_one[...]
    unit, inverse = norm_forward(normed + ffn + branch)
    dy = s.cotangent[rows, :].astype(F32)
    s.output[rows, :] = (unit * s.gain_two[...] + s.bias_two[...]).astype(BF16)
    add_vector(s, 2, jnp.sum(dy * unit, axis=0, keepdims=True))
    add_vector(s, 3, jnp.sum(dy, axis=0, keepdims=True))
    dh = norm_backward(dy, unit, inverse, s.gain_two[...])
    s.total[rows, :] = dh
    da = dh.astype(BF16)
    yield
    back = dot(da, s.up_two[...], NT)
    s.grads[3, :, :] += dot(act, da, TN)
    yield
    dz = (back * slope).astype(BF16)
    s.dffn[rows, :] = (dh + dot(dz, s.down_two[...])).astype(BF16)
    s.grads[2, :, :] += dot(dz, ffn_low, TN)


def feed_backward(s):
    for tile in range(s.w_inner.shape[0]):
        for rows in blocks_of(s):
            du = dot(s.dffn[rows, :], s.w_outer[tile], NT) * s.slope[tile, rows, :].astype(F32)
            s.total[rows, :] += dot(du.astype(BF16), s.w_inner[tile], NT)


def first_norm_backward(s, rows):
    dy = s.total[rows, :]
    unit = s.unit_one[rows, :]
    add_vector(s, 0, jnp.sum(dy * unit, axis=0, keepdims=True))
    add_vector(s, 1, jnp.sum(dy, axis=0, keepdims=True))
    dh = norm_backward(dy, unit, s.inverse_one[rows, :], s.gain_one[...])
    if rows.start == 0:
        s.near_total[...] = dh
    else:
        s.total[rows, :] = dh
    da = dh.astype(BF16)
    yield
    back = dot(da, s.up_one[...], NT)
    s.grads[1, :, :] += dot(s.act_one[rows, :], da, TN)
    yield
    dz = (back * s.slope_one[rows, :]).astype(BF16)
    branch = dot(dz, s.down_one[...])
    s.grads[0, :, :] += dot(dz, s.out_low[rows, :], TN)
    yield
    dout = (dh + branch).astype(BF16)
    s.ctx[rows, :] = dot(dout, s.w_out[...], NT).astype(BF16)


def project_back(s, total, grads, target):
    weights = (s.w_query, s.w_key, s.w_value)
    rows = target.shape[0]
    for block in [pl.ds(at, min(BLOCK, rows)) for at in range(0, rows, BLOCK)]:
        grad = total[block, :]
        for which, weight in enumerate(weights):
            grad = grad + dot(grads[which, block, :], weight[...], NT)
        target[block, :] = grad.astype(BF16)


INPUTS = (
    "w_query", "w_key", "w_value", "w_out", "w_inner", "w_outer",
    "down_one", "up_one", "down_two", "up_two",
    "gain_one", "bias_one", "gain_two", "bias_two",
)
BIG = INPUTS[:6]


def layer_scratch(span, near, per, width, hidden, adapt):
    pairs, tiles = width // LANES, hidden // width
    v = pltpu.VMEM
    return {
        "v_w_query": v((width, width), BF16),
        "v_w_key": v((width, width), BF16),
        "v_w_value": v((width, width), BF16),
        "v_w_out": v((width, width), BF16),
        "v_w_inner": v((tiles, width, width), BF16),
        "v_w_outer": v((tiles, width, width), BF16),
        "all_query": v((per, pairs, span, LANES), BF16),
        "all_key": v((per, pairs, span, LANES), BF16),
        "all_value": v((per, pairs, span, LANES), BF16),
        "expo": v((2 * pairs, span, span), BF16),
        "inv": v((pairs, span, LANES), F32),
        "attn": v((pairs, span, LANES), F32),
        "ctx": v((span, width), BF16),
        "out_low": v((span, width), BF16),
        "act_one": v((span, adapt), BF16),
        "slope_one": v((span, adapt), F32),
        "unit_one": v((span, width), F32),
        "inverse_one": v((span, 1), F32),
        "normed_low": v((span, width), BF16),
        "slope": v((tiles, span, width), BF16),
        "total": v((span, width), F32),
        "dffn": v((span, width), BF16),
        "all_near_grads": v((per, 3, near, width), BF16),
        "all_near_total": v((per, near, width), F32),
        "far_grads": v((3, span - near, width), BF16),
    }


class Reduce:
    def __init__(self, s, side, parts, devices, me, refs):
        self.s, self.side = s, side
        self.half, self.pair = lax.rem(me, 2), me // 2
        self.pairs, self.outer = parts // 2, devices // GROUP
        place = lax.axis_index("dp")
        self.inner, self.group = lax.rem(place, GROUP), place // GROUP
        self.send, self.got_near, self.part, self.got_dp, self.got_far, self.full, self.sems = (
            ref.at[side] for ref in refs
        )
        self.near = {"seq": me + 1 - 2 * self.half}
        self.ring = [lax.rem(self.inner + k, GROUP) for k in range(GROUP)]
        self.across = [{"dp": self.group * GROUP + k} for k in self.ring]
        self.far = [
            {
                "seq": lax.rem(self.pair + k % self.pairs, self.pairs) * 2 + self.half,
                "dp": lax.rem(self.group + k // self.pairs, self.outer) * GROUP + self.inner,
            }
            for k in range(self.pairs * self.outer)
        ]

    def greeted(self):
        return [self.near, *self.across[1:], *self.far[1:]]

    def copies(self, stage):
        mine, theirs = self.half * GROUP, (1 - self.half) * GROUP
        if stage == 0:
            moves = [(self.send.at[pl.ds(theirs, GROUP)], self.got_near, self.near)]
        elif stage == 1:
            moves = [(self.part.at[self.ring[k]], self.got_dp.at[k], self.across[k]) for k in range(1, GROUP)]
        elif stage == 2:
            block = self.got_far.at[self.group * self.pairs + self.pair]
            moves = [(block, block, device) for device in self.far[1:]]
        elif stage == 3:
            block = self.full.at[mine + self.inner]
            moves = [(block, block, device) for device in self.across[1:]]
        else:
            block = self.full.at[pl.ds(mine, GROUP)]
            moves = [(block, block, self.near)]
        return [
            pltpu.make_async_remote_copy(
                src_ref=source,
                dst_ref=target,
                send_sem=self.sems.at[0, stage, k],
                recv_sem=self.sems.at[1, stage, k],
                device_id=device,
                device_id_type=MESH,
            )
            for k, (source, target, device) in enumerate(moves)
        ]

    def start(self, stage):
        for copy in self.copies(stage):
            copy.start()

    def finish(self, stage):
        for copy in self.copies(stage):
            copy.wait()

    def first(self):
        grads, vectors = self.s.grads, self.s.vectors
        adapt, width = grads.shape[1:]
        chunks, rows = self.send.shape[:2]
        for c in range(chunks):
            at = c * rows
            matrix = 2 * self.side + at // adapt
            self.send[c, :, :width] = grads[matrix, at % adapt : at % adapt + rows, :].astype(BF16)
            self.send[c, :, width:] = vectors[self.side, c].astype(BF16)
        self.start(0)

    def second(self):
        self.finish(0)
        total = self.send[pl.ds(self.half * GROUP, GROUP)].astype(F32) + self.got_near[...].astype(F32)
        self.part[...] = total.astype(BF16)
        self.start(1)

    def third(self):
        self.finish(1)
        total = self.part[self.inner].astype(F32)
        for k in range(1, GROUP):
            total = total + self.got_dp[k].astype(F32)
        self.got_far[self.group * self.pairs + self.pair] = total.astype(BF16)
        self.start(2)

    def fourth(self):
        self.finish(2)
        total = self.got_far[0].astype(F32)
        for k in range(1, self.pairs * self.outer):
            total = total + self.got_far[k].astype(F32)
        self.full[self.half * GROUP + self.inner] = total.astype(BF16)
        self.start(3)

    def fifth(self):
        self.finish(3)
        self.start(4)


def layer_kernel(parts, devices, per, lengths, tokens, cotangent, *refs):
    s = Refs()
    refs = list(refs)
    for name in INPUTS:
        setattr(s, name, refs.pop(0))
    for name in INPUTS[10:]:
        setattr(s, name, getattr(s, name)[...].reshape(1, -1))
    hbm = {name: getattr(s, name) for name in BIG}
    output, grad_in, full = (refs.pop(0) for _ in range(3))
    for name in layer_scratch(LANES, 8, 1, LANES, LANES, 8):
        setattr(s, name, refs.pop(0))
    s.grads, s.vectors, x_in, dy_in = (refs.pop(0) for _ in range(4))
    w_sem, own_sem, send_sem, recv_sem = (refs.pop(0) for _ in range(4))

    me = lax.axis_index("seq")
    rows = tokens.shape[1]
    couples = parts // 2
    core, couple = lax.rem(me, 2), me // 2
    s.near_rows = 2 * rows
    s.shifts = []
    for k in range(couples):
        s.shifts.append((k * 2 * rows, (lax.rem(couple + k, couples) - k) * 2 * rows))
    near = [(0, 1 - core)]
    far = [(k, c) for c in range(2) for k in range(1, couples)]

    def index_of(peer):
        k, c = peer
        return lax.rem(couple + k, couples) * 2 + c

    refs.insert(5, full)
    one, two = (Reduce(s, side, parts, devices, me, refs) for side in range(2))

    barrier = pltpu.get_barrier_semaphore()
    greeted = [{"seq": index_of(peer)} for peer in near + far] + one.greeted()
    for device in greeted:
        pl.semaphore_signal(barrier, inc=1, device_id=device, device_id_type=MESH)

    width = tokens.shape[2]
    weight_copies = []
    for index, name in enumerate(BIG):
        ref = getattr(s, "v_" + name)
        if name == "w_inner":
            for t in range(ref.shape[0]):
                weight_copies.append(
                    pltpu.make_async_copy(hbm[name].at[:, pl.ds(t * width, width)], ref.at[t], w_sem.at[index, t])
                )
        elif name == "w_outer":
            for t in range(ref.shape[0]):
                weight_copies.append(
                    pltpu.make_async_copy(hbm[name].at[pl.ds(t * width, width), :], ref.at[t], w_sem.at[index, t])
                )
        else:
            weight_copies.append(pltpu.make_async_copy(hbm[name], ref, w_sem.at[index, 0]))
        setattr(s, name, ref)

    pl.semaphore_wait(barrier, len(greeted))

    def move(array, step, peer, slot):
        k, c = (0, core) if peer is None else peer
        other = me if peer is None else index_of(peer)
        outside, inside = ((tokens, x_in), (cotangent, dy_in), (output, dy_in), (grad_in, x_in))[array]
        if array < 2:
            source = outside.at[step * parts + other]
            target = inside.at[step, pl.ds((couples - k) % couples * 2 * rows + core * rows, rows)]
        else:
            source = inside.at[step, pl.ds(k * 2 * rows + c * rows, rows)]
            target = outside.at[step * parts + me]
        if peer is None:
            return pltpu.make_async_copy(source, target, own_sem.at[array, step])
        return pltpu.make_async_remote_copy(
            src_ref=source,
            dst_ref=target,
            send_sem=send_sem.at[array, step, other],
            recv_sem=recv_sem.at[array, step, other if slot is None else slot],
            device_id={"seq": other},
            device_id_type=MESH,
        )

    def start(array, step, peers):
        for peer in peers:
            move(array, step, peer, me).start()

    def finish(array, step, peers):
        for peer in peers:
            move(array, step, peer, None).wait()

    near = near + [None]
    everyone = far + near

    def view(step):
        s.tokens, s.cotangent = x_in.at[step], dy_in.at[step]
        s.query, s.key, s.value = (ref.at[step] for ref in (s.all_query, s.all_key, s.all_value))
        s.near_grads, s.near_total = s.all_near_grads.at[step], s.all_near_total.at[step]
        s.output = s.cotangent
        s.length = lengths[step * parts + me]

    near_rows, far_rows = pl.ds(0, s.near_rows), pl.ds(s.near_rows, x_in.shape[1] - s.near_rows)
    start(0, 0, far)
    for step in range(per):
        start(0, step, near)
    for copy in weight_copies:
        copy.start()
    for ref in (s.grads, s.vectors):
        ref[...] = jnp.zeros_like(ref)
    for copy in weight_copies[:3]:
        copy.wait()

    @pl.loop(0, per)
    def _(step):
        view(step)
        finish(0, step, near)
        project_in(s, [near_rows])

    for copy in weight_copies[3:]:
        copy.wait()

    @pl.loop(0, per)
    def _(step):
        more, final = step + 1 < per, step == per - 1
        view(step)
        finish(0, step, far)

        @pl.when(step == 0)
        def _():
            start(1, 0, everyone)

        @pl.when(more)
        def _():
            start(0, step + 1, far)

        project_in(s, far_blocks(s))
        attend_forward(s)
        first_norm(s)
        feed_forward(s)
        finish(1, step, everyone)

        @pl.when(more)
        def _():
            start(1, step + 1, everyone)

        at_end = pl.when(final)
        lockstep(second_norm(s, block) for block in blocks_of(s))
        start(2, step, everyone)
        feed_backward(s)
        lockstep(first_norm_backward(s, block) for block in [near_rows, *far_blocks(s)])

        @at_end
        def _():
            two.first()
            one.first()
            two.second()
            one.second()

        for pair in range(s.query.shape[0]):
            attend_backward(s, pair)

        @at_end
        def _():
            two.third()
            one.third()

        project_back(s, s.total.at[far_rows], s.far_grads, x_in.at[step, far_rows])
        start(3, step, far)

    for step in range(per):
        view(step)
        project_back(s, s.near_total, s.near_grads, x_in.at[step, near_rows])
        start(3, step, near)
        if step == 0:
            two.fourth()
            one.fourth()
        if step == per - 1:
            two.fifth()
            one.fifth()
    one.finish(4)
    two.finish(4)

    @pl.loop(0, per)
    def _(step):
        finish(2, step, everyone)
        finish(3, step, everyone)


def tail_kernel(output, grad_in, full, output_out, grad_in_out, *grads):
    output_out[...] = output[...]
    grad_in_out[...] = grad_in[...].astype(F32)

    @pl.when(pl.program_id(0) == 0)
    def _():
        matrices, vectors = grads[:4], grads[4:]
        adapt, width = matrices[0].shape
        chunks, rows = full.shape[1:3]
        for side in range(2):
            for c in range(chunks):
                at = c * rows
                matrix = matrices[2 * side + at // adapt]
                matrix[at % adapt : at % adapt + rows, :] = full[side, c, :, :width].astype(F32)
        tails = full[:, :, :, width:].astype(F32)
        for vector, piece, side, chunk, row in vector_slots(width):
            vectors[vector][pair_lanes(piece)] = tails[side, chunk, row]


def per_device(parts, devices, tokens, lengths, cotangent, *params):
    batch, rows, width = tokens.shape
    hidden, adapt = params[4].shape[1], params[6].shape[1]
    per, span = batch // parts, parts * rows
    chunks, chunk_rows = 2 * GROUP, adapt // GROUP
    far = parts // 2 * (devices // GROUP)
    params = list(params)
    params[6], params[8] = params[6].T, params[8].T
    vmem = pl.BlockSpec(memory_space=pltpu.VMEM)
    anywhere = pl.BlockSpec(memory_space=pl.ANY)
    dma = pltpu.SemaphoreType.DMA
    chunk = (chunk_rows, width + LANES)
    scratch = [
        *layer_scratch(span, 2 * rows, per, width, hidden, adapt).values(),
        pltpu.VMEM((4, adapt, width), F32),
        pltpu.VMEM((2, chunks, chunk_rows, LANES), F32),
        *[pltpu.VMEM((per, span, width), BF16)] * 2,
        dma((len(BIG), hidden // width)),
        dma((4, per)),
        dma((4, per, parts)),
        dma((4, per, parts)),
        pltpu.VMEM((2, chunks, *chunk), BF16),
        *[pltpu.VMEM((2, GROUP, *chunk), BF16)] * 3,
        pltpu.VMEM((2, far, *chunk), BF16),
        dma((2, 2, 5, max(GROUP, far))),
    ]
    moved = jax.ShapeDtypeStruct((batch, rows, width), BF16)
    summed = jax.ShapeDtypeStruct((2, chunks, *chunk), BF16)
    output, grad_in, full = pl.pallas_call(
        functools.partial(layer_kernel, parts, devices, per),
        out_shape=(moved, moved, summed),
        in_specs=[pl.BlockSpec(memory_space=pltpu.SMEM)]
        + [anywhere] * 2
        + [anywhere if name in BIG else vmem for name in INPUTS],
        out_specs=(anywhere, anywhere, vmem),
        scratch_shapes=scratch,
        compiler_params=pltpu.CompilerParams(
            collective_id=0, has_side_effects=True, vmem_limit_bytes=62 * 2**20
        ),
        name="layer",
    )(lengths, tokens, cotangent, *params)
    block = pl.BlockSpec((batch // 2, rows, width), lambda i: (i, 0, 0))
    whole = [pl.BlockSpec((adapt, width), lambda i: (0, 0))] * 4 + [pl.BlockSpec((width,), lambda i: (0,))] * 4
    output, grad_in, down_one, up_one, down_two, up_two, *vectors = pl.pallas_call(
        tail_kernel,
        grid=(2,),
        out_shape=(
            moved,
            jax.ShapeDtypeStruct((batch, rows, width), F32),
            *[jax.ShapeDtypeStruct((adapt, width), F32)] * 4,
            *[jax.ShapeDtypeStruct((width,), F32)] * 4,
        ),
        in_specs=[block, block, pl.BlockSpec(summed.shape, lambda i: (0, 0, 0, 0))],
        out_specs=(block, block, *whole),
        name="tail",
    )(output, grad_in, full)
    return (output, grad_in, down_one.T, up_one, down_two.T, up_two, *vectors)


def solution(mesh):
    split = P("dp", "seq", None)
    return jax.shard_map(
        functools.partial(per_device, mesh.shape["seq"], mesh.shape["dp"]),
        mesh=mesh,
        in_specs=(split, P("dp"), split) + (P(),) * 14,
        out_specs=(split, split) + (P(),) * 8,
        check_vma=False,
    )
```
